32 devices in a mesh: grp: 2 (over y), tile: 4 (over z), kern: 4 (over x, core).
Axes of the slice: x: 2, y: 2, z: 4, core: 2. Of those that a mesh axis runs over, the one named last changes fastest.
Arguments:
- mask_theta: float32 [6, 1024, 1024], P('grp', 'tile', 'kern'), parts along dimension 0, may hold values from -6 to 6
- first_moment: float32 [6, 1024, 1024], P('grp', 'tile', 'kern'), parts along dimension 0, may hold values from -1.5 to 1.5
- second_moment: float32 [6, 1024, 1024], P('grp', 'tile', 'kern'), parts along dimension 0, may hold values from 0.0001 to 0.01
- target_bits: int32 [6, 1024, 36], P('grp', 'tile', 'kern'), parts along dimension 0, may hold values from 0 to 1073741823
- kernels: float32 [2, 16, 128, 128], P(None, 'kern'), may hold values from -6 to 6
- kernel_weights: float32 [16], P('kern'), may hold values from 0.02 to 0.2
Outputs:
- updated_theta: float32 [6, 1024, 1024], P('grp', 'tile', 'kern'), parts along dimension 0
- updated_first: float32 [6, 1024, 1024], P('grp', 'tile', 'kern'), parts along dimension 0
- updated_second: float32 [6, 1024, 1024], P('grp', 'tile', 'kern'), parts along dimension 0
- gradient: float32 [6, 1024, 1024], P('grp', 'tile', 'kern'), parts along dimension 0
The draws below stay inside these ranges and needn't reach their ends.
There are 2 independent parts, one for each index of `grp`. The reference program is written for one: setup_inputs(seed, part) draws one part's arguments, and reference() takes and returns one part's arrays. A program takes and returns all parts, laid end to end along the dimension named above; an argument that names none is the same for every part. Nothing has to cross between parts.
Inputs may be any that keep to these rules, and one draw needn't show every extreme that they name: `target_bits`: bit j (j < 30) of word q * 9 + w of a row is the target of pixel column q * 256 + 30 w + j; bits for columns at or past (q + 1) * 256 are ignored.
All inputs are finite; a program needn't handle non-finite values.
Results may differ from the reference program's by a relative error of at most 0.04.
Values may be sent and summed in bfloat16 or wider, within the bound.
No kernel may reach another device: no remote copies, remote signals or barrier semaphores. Data moves between devices by JAX's collectives and lax.ppermute only.
A program may use at most 192 MiB of HBM per device.

```python
import math
import jax
import jax.numpy as jnp
from jax import lax

PIXELS = 1024
BAND = 128
KERNELS = 16
TILES = 3
ITERS = 4
COLS_DEV = 256
WORDS_DEV = 9
WORDS = 36
N_KERN = 4


def touch_ends(result, stream_key, least, high):
    index_at = [jax.random.randint(jax.random.fold_in(stream_key, axis), (), 0, length) for axis, length in enumerate(result.shape)]
    longest = result.shape.index(max(result.shape))
    neighbour = index_at[:longest] + [(index_at[longest] + 1) % result.shape[longest]] + index_at[longest + 1:]
    return result.at[tuple(index_at)].set(least).at[tuple(neighbour)].set(high)


def block_scale(key, shape, shards, smallest, largest):
    level, own = 1.0, jax.random.fold_in(key, 6)
    for axis_at, shards_of in shards:
        heights = jnp.exp(jax.random.uniform(jax.random.fold_in(own, axis_at), (shards_of,), jnp.float32, smallest / len(shards), largest / len(shards)))
        level = level * jnp.repeat(heights, shape[axis_at] // shards_of).reshape([-1 if axis == axis_at else 1 for axis in range(len(shape))])
    return level


def noise(rng, extent, scale, bound, split=(), kind=jnp.bfloat16):
    drawn = scale * jax.random.normal(rng, extent, jnp.float32)
    if split:
        drawn = drawn * block_scale(rng, extent, split, -0.22, 0.18)
    return jnp.clip(drawn, -bound, bound).astype(kind)


def setup_inputs(seed: int = 0, part: int = 0) -> dict:
    splits = jax.random.split(jax.random.key(seed), 7)
    part_keys = jax.random.split(jax.random.fold_in(splits[6], part), 7)
    return {
        "mask_theta": noise(part_keys[0], (TILES, PIXELS, PIXELS), 1.0, 6.0, ((1, 4), (2, 4)), jnp.float32),
        "first_moment": noise(part_keys[1], (TILES, PIXELS, PIXELS), 0.1, 1.5, ((1, 4), (2, 4)), jnp.float32),
        "second_moment": jnp.clip(jnp.exp(math.log(0.01) - 4.6051702 * jax.random.uniform(part_keys[2], (TILES, PIXELS, PIXELS), jnp.float32) ** block_scale(part_keys[2], (TILES, PIXELS, PIXELS), ((1, 4), (2, 4)), -0.2, 0.2)), 0.0001, 0.01),
        "target_bits": touch_ends(jax.random.randint(part_keys[3], (TILES, PIXELS, WORDS), 0, 2 ** 30), jax.random.fold_in(part_keys[3], 1), 0, (2 ** 30) - 1).astype(jnp.int32),
        "kernels": noise(splits[4], (2, KERNELS, BAND, BAND), 1.0, 6.0, ((1, 4),), jnp.float32),
        "kernel_weights": jnp.clip(jnp.exp(math.log(0.2) - 2.3025851 * jax.random.uniform(splits[5], (KERNELS,), jnp.float32) ** block_scale(splits[5], (KERNELS,), ((0, 4),), -0.2, 0.2)), 0.02, 0.2),
    }


learn_rate = 0.1
beta_one = 0.9
beta_two = 0.999
adam_eps = 1e-08
first_step = 10
resist_gain = 3.0
resist_level = 1.0

def tables(band_count, length, offset):
    frequencies = jnp.arange(band_count, dtype=jnp.int32) - band_count // 2
    places = jnp.arange(length, dtype=jnp.int32) + offset
    phases = frequencies[:, None] * places[None, :] % PIXELS
    angles = phases.astype(jnp.float32) * (2.0 * math.pi / PIXELS)
    return (jnp.cos(angles).astype(jnp.bfloat16), jnp.sin(angles).astype(jnp.bfloat16))

def unpack(packed_words, column_count):
    shifts = jnp.arange(30, dtype=jnp.int32)
    bit_values = jnp.right_shift(packed_words[..., None], shifts) & 1
    flat_bits = bit_values.reshape(packed_words.shape[:-1] + (packed_words.shape[-1] * 30,))
    return flat_bits[..., :column_count]

def pattern_drive(intensity, target):
    resist = jax.nn.sigmoid(resist_gain * (intensity - resist_level))
    return (2.0 * resist_gain * (resist - target) * resist * (1.0 - resist)).astype(jnp.bfloat16)

def adam_update(theta_cur, moment_one, moment_two, gradient, step_number):
    fix_one = 1.0 - beta_one ** step_number
    fix_two = 1.0 - beta_two ** step_number
    new_first = beta_one * moment_one + (1.0 - beta_one) * gradient
    new_second = beta_two * moment_two + (1.0 - beta_two) * gradient * gradient
    new_theta = theta_cur - learn_rate * (new_first / fix_one) / (jnp.sqrt(new_second / fix_two) + adam_eps)
    return (new_theta, new_first, new_second)

def product(einsum_form, left_side, right_side):
    return jnp.einsum(einsum_form, left_side.astype(jnp.float32), right_side.astype(jnp.float32), precision=lax.Precision.HIGHEST)

def image_field(spectrum_real, spectrum_imag, kernel_real, kernel_imag, cosine, sine_table):
    pupil_real = (kernel_real * spectrum_real - kernel_imag * spectrum_imag).astype(jnp.bfloat16)
    pupil_imag = (kernel_real * spectrum_imag + kernel_imag * spectrum_real).astype(jnp.bfloat16)
    half_real = (product('bx,tbc->txc', cosine, pupil_real) - product('bx,tbc->txc', sine_table, pupil_imag)).astype(jnp.bfloat16)
    half_imag = (product('bx,tbc->txc', cosine, pupil_imag) + product('bx,tbc->txc', sine_table, pupil_real)).astype(jnp.bfloat16)
    field_real = (product('txc,cy->txy', half_real, cosine) - product('txc,cy->txy', half_imag, sine_table)) / BAND
    field_imag = (product('txc,cy->txy', half_real, sine_table) + product('txc,cy->txy', half_imag, cosine)) / BAND
    return (field_real, field_imag)

def reference(mask_theta, first_moment, second_moment, target_bits, kernels, kernel_weights):
    cosine, sine_table = tables(BAND, PIXELS, 0)
    block_words = target_bits.reshape(TILES, PIXELS, N_KERN, WORDS_DEV)
    target = unpack(block_words, COLS_DEV).reshape(TILES, PIXELS, PIXELS).astype(jnp.float32)
    theta_cur = mask_theta
    moment_one = first_moment
    moment_two = second_moment
    gradient = jnp.zeros_like(mask_theta)
    for iteration in range(ITERS):
        mask_bf = jnp.tanh(theta_cur).astype(jnp.bfloat16)
        across_cosine = product('txy,by->txb', mask_bf, cosine).astype(jnp.bfloat16)
        across_sine = product('txy,by->txb', mask_bf, sine_table).astype(jnp.bfloat16)
        spectrum_real = (product('bx,txc->tbc', cosine, across_cosine) - product('bx,txc->tbc', sine_table, across_sine)) / PIXELS
        spectrum_imag = -(product('bx,txc->tbc', sine_table, across_cosine) + product('bx,txc->tbc', cosine, across_sine)) / PIXELS

        def add_intensity(totals, stacked):
            kernel_real, kernel_imag, weight = stacked
            field_real, field_imag = image_field(spectrum_real, spectrum_imag, kernel_real, kernel_imag, cosine, sine_table)
            return (totals + weight * (field_real * field_real + field_imag * field_imag), None)
        intensity, unused = lax.scan(add_intensity, jnp.zeros((TILES, PIXELS, PIXELS), jnp.float32), (kernels[0], kernels[1], kernel_weights))
        pattern_grad = pattern_drive(intensity, target)

        def add_adjoint(totals, stacked):
            kernel_real, kernel_imag, weight = stacked
            field_real, field_imag = image_field(spectrum_real, spectrum_imag, kernel_real, kernel_imag, cosine, sine_table)
            real_bf = field_real.astype(jnp.bfloat16)
            imag_bf = field_imag.astype(jnp.bfloat16)
            drive_term = 2.0 * weight * pattern_grad.astype(jnp.float32)
            push_real = (drive_term * real_bf.astype(jnp.float32)).astype(jnp.bfloat16)
            push_imag = (drive_term * imag_bf.astype(jnp.float32)).astype(jnp.bfloat16)
            back_real = (product('txy,by->txb', push_real, cosine) + product('txy,by->txb', push_imag, sine_table)).astype(jnp.bfloat16)
            back_imag = (product('txy,by->txb', push_imag, cosine) - product('txy,by->txb', push_real, sine_table)).astype(jnp.bfloat16)
            spectral_real = (product('bx,txc->tbc', cosine, back_real) + product('bx,txc->tbc', sine_table, back_imag)) / BAND
            spectral_imag = (product('bx,txc->tbc', cosine, back_imag) - product('bx,txc->tbc', sine_table, back_real)) / BAND
            return ((totals[0] + (kernel_real * spectral_real + kernel_imag * spectral_imag), totals[1] + (kernel_real * spectral_imag - kernel_imag * spectral_real)), None)
        zero_spectrum = jnp.zeros((TILES, BAND, BAND), jnp.float32)
        adjoint_pair, unused = lax.scan(add_adjoint, (zero_spectrum, zero_spectrum), (kernels[0], kernels[1], kernel_weights))
        adjoint_real_bf = adjoint_pair[0].astype(jnp.bfloat16)
        adjoint_imag_bf = adjoint_pair[1].astype(jnp.bfloat16)
        rows_real = (product('bx,tbc->txc', cosine, adjoint_real_bf) - product('bx,tbc->txc', sine_table, adjoint_imag_bf)).astype(jnp.bfloat16)
        rows_imag = (product('bx,tbc->txc', cosine, adjoint_imag_bf) + product('bx,tbc->txc', sine_table, adjoint_real_bf)).astype(jnp.bfloat16)
        mask_grad = (product('txc,cy->txy', rows_real, cosine) - product('txc,cy->txy', rows_imag, sine_table)) / PIXELS
        gradient = mask_grad * (1.0 - jnp.tanh(theta_cur) ** 2)
        theta_cur, moment_one, moment_two = adam_update(theta_cur, moment_one, moment_two, gradient, first_step + iteration)
    return (theta_cur, moment_one, moment_two, gradient)
```

```python
import functools

import jax
import jax.numpy as jnp
import numpy as np
from jax import lax
from jax.experimental import pallas as pl
from jax.experimental.pallas import tpu as pltpu
from jax.sharding import PartitionSpec as P

ITERS = 4
GROUPS = (3,)

learn_rate = 0.1
beta_one = 0.9
beta_two = 0.999
adam_eps = 1e-08
first_step = 10
resist_gain = 3.0
resist_level = 1.0

BF = jnp.bfloat16
F32 = jnp.float32


def dot(left, right):
    return jnp.dot(left, right, preferred_element_type=F32)


def cos_sin(band, pixels, places):
    freq = np.arange(band, dtype=np.int64) - band // 2
    phase = (freq[None, :] * np.asarray(places, np.int64)[:, None]) % pixels
    angle = phase * (2.0 * np.pi / pixels)
    return np.concatenate([np.cos(angle), np.sin(angle)], axis=1)


def interpolation(coarse, pixels):
    step = pixels // coarse
    offset = (np.arange(pixels)[:, None] - step * np.arange(coarse)[None, :]) % pixels
    freq = np.arange(1, coarse // 2)
    kernel = 1.0 + 2.0 * np.cos(
        2.0 * np.pi * ((freq[None, :] * np.arange(pixels)[:, None]) % pixels) / pixels
    ).sum(axis=1)
    return kernel[offset] / coarse


def for_each(count, step):
    if count == 1:
        step(0)
    else:
        lax.fori_loop(0, count, lambda i, c: (step(i), c)[1], 0)


def call(body, out_shape, args, scratch=(), flops=0):
    vmem = pl.BlockSpec(memory_space=pltpu.VMEM)
    many = isinstance(out_shape, (list, tuple))
    nbytes = sum(int(np.prod(a.shape)) * a.dtype.itemsize for a in args)
    return pl.pallas_call(
        body,
        out_shape=out_shape,
        in_specs=[vmem] * len(args),
        out_specs=[vmem] * len(out_shape) if many else vmem,
        scratch_shapes=list(scratch),
        cost_estimate=pl.CostEstimate(flops=flops, bytes_accessed=nbytes, transcendentals=0),
    )(*args)


def unpack_kernel(words_ref, target_ref):
    count, rows, columns = target_ref.shape
    word_count = words_ref.shape[2]
    lane = lax.broadcasted_iota(jnp.int32, (rows, columns), 1)
    place = lane // 30
    shift = lane - 30 * place

    def image(i):
        words = words_ref[i]
        picked = jnp.broadcast_to(words[:, 0:1], (rows, columns))
        for w in range(1, word_count):
            picked = jnp.where(place == w, words[:, w : w + 1], picked)
        bits = jnp.right_shift(picked, shift) & 1
        target_ref[i] = bits.astype(F32).astype(BF)

    for_each(count, image)


def spectrum_part(theta, across_y, down_x, band, pixels):
    mask_bf = jnp.tanh(theta).astype(BF)
    across = dot(mask_bf, across_y).astype(BF)
    part = dot(down_x, across) * (1.0 / pixels)
    real = part[:band, :band] - part[band:, band:]
    imag = -(part[band:, :band] + part[:band, band:])
    return real.astype(BF), imag.astype(BF)


def mask_kernel(band, pixels, theta_ref, across_y_ref, down_x_ref, out_ref):
    def image(i):
        real, imag = spectrum_part(theta_ref[i], across_y_ref[...], down_x_ref[...], band, pixels)
        out_ref[0, i] = real
        out_ref[1, i] = imag

    for_each(theta_ref.shape[0], image)


def update_kernel(
    band,
    pixels,
    step_number,
    last,
    adjoint_ref,
    theta_ref,
    first_ref,
    second_ref,
    along_x_ref,
    onto_y_ref,
    across_y_ref,
    down_x_ref,
    new_theta_ref,
    new_first_ref,
    new_second_ref,
    out_ref,
):
    fix_one = 1.0 - beta_one**step_number
    fix_two = 1.0 - beta_two**step_number

    def image(i):
        real, imag = adjoint_ref[0, i], adjoint_ref[1, i]
        square = jnp.concatenate(
            [jnp.concatenate([real, imag], axis=1), jnp.concatenate([-imag, real], axis=1)], axis=0
        )
        rows = dot(along_x_ref[...], square).astype(BF)
        mask_grad = dot(rows, onto_y_ref[...]) * (1.0 / pixels)
        theta = theta_ref[i]
        gradient = mask_grad * (1.0 - jnp.tanh(theta) ** 2)
        new_first = beta_one * first_ref[i] + (1.0 - beta_one) * gradient
        new_second = beta_two * second_ref[i] + (1.0 - beta_two) * gradient * gradient
        new_theta = theta - learn_rate * (new_first / fix_one) / (
            jnp.sqrt(new_second / fix_two) + adam_eps
        )
        new_theta_ref[i] = new_theta
        new_first_ref[i] = new_first
        new_second_ref[i] = new_second
        if last:
            out_ref[i] = gradient
        else:
            part_real, part_imag = spectrum_part(
                new_theta, across_y_ref[...], down_x_ref[...], band, pixels
            )
            out_ref[0, i] = part_real
            out_ref[1, i] = part_imag

    for_each(theta_ref.shape[0], image)


def field_kernel(
    spectrum_ref, kernels_ref, rows_ref, columns_ref, fields_ref, intensity_ref, total_ref
):
    kernel_count = kernels_ref.shape[1]
    coarse = rows_ref.shape[0]

    def image(i):
        spectrum_real = spectrum_ref[0, i].astype(F32)
        spectrum_imag = spectrum_ref[1, i].astype(F32)

        def one(k, carry):
            kernel_real = kernels_ref[0, k].astype(F32)
            kernel_imag = kernels_ref[1, k].astype(F32)
            real = (kernel_real * spectrum_real - kernel_imag * spectrum_imag).astype(BF)
            imag = (kernel_real * spectrum_imag + kernel_imag * spectrum_real).astype(BF)
            square = jnp.concatenate(
                [
                    jnp.concatenate([real, imag], axis=1),
                    jnp.concatenate([-imag, real], axis=1),
                ],
                axis=0,
            )
            half = dot(rows_ref[...], square).astype(BF)
            field = dot(half, columns_ref[...])
            fields_ref[i, k] = field.astype(BF)
            field_real, field_imag = field[:, :coarse], field[:, coarse:]
            power = field_real * field_real + field_imag * field_imag

            @pl.when(k == 0)
            def _():
                total_ref[...] = power

            @pl.when(k > 0)
            def _():
                total_ref[...] += power

            return carry

        lax.fori_loop(0, kernel_count, one, 0)
        intensity_ref[i] = total_ref[...].astype(BF)

    for_each(fields_ref.shape[0], image)


def resist_kernel(
    own_ref,
    other_ref,
    target_ref,
    up_x_ref,
    down_x_ref,
    up_y_ref,
    down_y_ref,
    out_ref,
):
    pixels, coarse = up_x_ref.shape
    chunk = min(256, pixels)

    def image(i):
        intensity = (own_ref[i].astype(F32) + other_ref[i].astype(F32)).astype(BF)
        wide = dot(intensity, up_y_ref[...]).astype(BF)
        total = None
        for start in range(0, pixels, chunk):
            fine = dot(up_x_ref[start : start + chunk, :], wide)
            resist = jax.nn.sigmoid(resist_gain * (fine - resist_level))
            target = target_ref[i, start : start + chunk, :].astype(F32)
            drive = 2.0 * resist_gain * (resist - target) * resist * (1.0 - resist)
            term = dot(down_x_ref[:, start : start + chunk], drive.astype(BF))
            total = term if total is None else total + term
        out_ref[i] = dot(total.astype(BF), down_y_ref[...]).astype(BF)

    for_each(own_ref.shape[0], image)


def adjoint_kernel(
    own_ref, other_ref, fields_ref, kernels_ref, columns_ref, rows_ref, out_ref, real_ref, imag_ref
):
    kernel_count = kernels_ref.shape[1]
    band = kernels_ref.shape[3]
    coarse = own_ref.shape[2]

    def image(i):
        drive = (own_ref[i].astype(F32) + other_ref[i].astype(F32)).astype(BF)
        drive_twice = jnp.concatenate([drive, drive], axis=1)
        real_ref[...] = jnp.zeros_like(real_ref)
        imag_ref[...] = jnp.zeros_like(imag_ref)

        def one(k, carry):
            push = drive_twice * fields_ref[i, k]
            back = dot(push, columns_ref[...]).astype(BF)
            parts = dot(rows_ref[...], back)
            spectral_real = parts[:band, :band] + parts[band:, band:]
            spectral_imag = parts[:band, band:] - parts[band:, :band]
            kernel_real = kernels_ref[0, k].astype(F32)
            kernel_imag = kernels_ref[1, k].astype(F32)
            real_ref[...] += kernel_real * spectral_real + kernel_imag * spectral_imag
            imag_ref[...] += kernel_real * spectral_imag - kernel_imag * spectral_real
            return carry

        lax.fori_loop(0, kernel_count, one, 0)
        out_ref[0, i] = real_ref[...].astype(BF)
        out_ref[1, i] = imag_ref[...].astype(BF)

    for_each(own_ref.shape[0], image)


def swap(value, axis, mask):
    count = lax.axis_size(axis)
    return lax.ppermute(value, axis, [(i, i ^ mask) for i in range(count)])


def add(first, *others):
    total = first.astype(F32)
    for other in others:
        total = total + other.astype(F32)
    return total.astype(BF)


def sum_axis(value, axis, unit, count):
    if count <= 4:
        return add(value, *[swap(value, axis, unit * m) for m in range(1, count)])
    bit = 1
    while bit < count:
        value = add(value, swap(value, axis, unit * bit))
        bit *= 2
    return value


def sum_all(value, core, chips, tiles):
    mine = lax.dynamic_index_in_dim(value, core, 0, keepdims=False)
    theirs = lax.dynamic_index_in_dim(value, 1 - core, 0, keepdims=False)
    mine = add(mine, swap(theirs, "kern", 1))
    mine = sum_axis(mine, "kern", 2, chips)
    mine = sum_axis(mine, "tile", 1, tiles)
    other = swap(mine, "kern", 1)
    real = jnp.where(core == 0, mine, other)
    imag = jnp.where(core == 0, other, mine)
    return jnp.stack([real, imag])


def sum_kern(value, chips):
    value = add(value, swap(value, "kern", 1))
    return sum_axis(value, "kern", 2, chips)


def body(mask_theta, first_moment, second_moment, target_bits, kernels, kernel_weights):
    tile_count, row_count, column_count = mask_theta.shape
    band = kernels.shape[-1]
    coarse = 2 * band
    tiles = lax.axis_size("tile")
    chips = lax.axis_size("kern") // 2
    pixels = tiles * row_count
    step = pixels // coarse
    tile_at = lax.axis_index("tile")
    kern_at = lax.axis_index("kern")
    core = kern_at % 2

    fine = cos_sin(band, pixels, np.arange(pixels))
    fine_table = jnp.asarray(fine, BF)
    fine_table_t = jnp.asarray(fine.T, BF)
    signed_t = jnp.asarray(np.concatenate([fine.T[:band], -fine.T[band:]]), BF)
    up = interpolation(coarse, pixels)
    up_table = jnp.asarray(up, BF)
    up_table_t = jnp.asarray(up.T, BF)
    coarse_rows = fine[::step]
    cos_c, sin_c = coarse_rows[:, :band], coarse_rows[:, band:]
    field_rows = jnp.asarray(coarse_rows, BF)
    field_columns = jnp.asarray(
        np.block([[cos_c.T, sin_c.T], [-sin_c.T, cos_c.T]]) / band, BF
    )
    back_columns = jnp.asarray(np.block([[cos_c, -sin_c], [sin_c, cos_c]]) * (2.0 / band), BF)
    back_rows = jnp.asarray(coarse_rows.T, BF)

    row_start = tile_at * row_count
    column_start = kern_at * column_count
    along_x = lax.dynamic_slice_in_dim(fine_table, row_start, row_count, 0)
    down_x = lax.dynamic_slice_in_dim(fine_table_t, row_start, row_count, 1)
    across_y = lax.dynamic_slice_in_dim(fine_table, column_start, column_count, 0)
    onto_y = lax.dynamic_slice_in_dim(signed_t, column_start, column_count, 1)
    up_y = lax.dynamic_slice_in_dim(up_table_t, column_start, column_count, 1)
    down_y = lax.dynamic_slice_in_dim(up_table, column_start, column_count, 0)

    scaled = (kernels * jnp.sqrt(kernel_weights)[None, :, None, None]).astype(BF)
    own_kernels = jnp.concatenate(
        [scaled] + [swap(scaled, "kern", 2 * m) for m in range(1, chips)], axis=1
    )
    word_blocks = jnp.stack(
        [target_bits] + [swap(target_bits, "tile", m) for m in range(1, tiles)]
    )
    word_blocks = jnp.take(word_blocks, jnp.arange(tiles, dtype=jnp.int32) ^ tile_at, axis=0)
    words = jnp.moveaxis(word_blocks, 0, 1).reshape(tile_count, pixels, target_bits.shape[2])

    groups, start = [], 0
    for size in GROUPS:
        groups.append(slice(start, start + size))
        start += size

    def spread(shape, dtype=BF):
        return jax.ShapeDtypeStruct(shape, dtype)

    results = []
    for group in groups:
        count = group.stop - group.start
        theta, first, second = mask_theta[group], first_moment[group], second_moment[group]
        block = spread(theta.shape, F32)
        target = call(
            unpack_kernel, spread((count, pixels, column_count)), (words[group],), flops=10**6
        )
        part = call(
            functools.partial(mask_kernel, band, pixels),
            spread((2, count, band, band)),
            (theta, across_y, down_x),
            flops=count * 10**8,
        )
        gradient = None
        for iteration in range(ITERS):
            spectrum = sum_all(part, core, chips, tiles)
            kernel_count = own_kernels.shape[1]
            fields, intensity = call(
                field_kernel,
                [
                    spread((count, kernel_count, coarse, 2 * coarse)),
                    spread((count, coarse, coarse)),
                ],
                (spectrum, own_kernels, field_rows, field_columns),
                scratch=[pltpu.VMEM((coarse, coarse), F32)],
                flops=count * 10**9,
            )
            drive = call(
                resist_kernel,
                spread((count, coarse, coarse)),
                (
                    intensity,
                    swap(intensity, "kern", 1),
                    target,
                    up_table,
                    up_table_t,
                    up_y,
                    down_y,
                ),
                flops=count * 4 * 10**8,
            )
            adjoint = call(
                adjoint_kernel,
                spread((2, count, band, band)),
                (drive, swap(drive, "kern", 1), fields, own_kernels, back_columns, back_rows),
                scratch=[pltpu.VMEM((band, band), F32)] * 2,
                flops=count * 10**9,
            )
            adjoint = sum_kern(adjoint, chips)
            last = iteration == ITERS - 1
            theta, first, second, out = call(
                functools.partial(update_kernel, band, pixels, first_step + iteration, last),
                [block, block, block, block if last else spread((2, count, band, band))],
                (adjoint, theta, first, second, along_x, onto_y, across_y, down_x),
                flops=count * 2 * 10**8,
            )
            if last:
                gradient = out
            else:
                part = out
        results.append((theta, first, second, gradient))
    return tuple(jnp.concatenate(parts) if len(parts) > 1 else parts[0] for parts in zip(*results))


def solution(mesh):
    block = P("grp", "tile", "kern")
    return jax.shard_map(
        body,
        mesh=mesh,
        in_specs=(block, block, block, block, P(None, "kern", None, None), P("kern")),
        out_specs=(block, block, block, block),
        check_vma=False,
    )
```

```python
import functools

import jax
import jax.numpy as jnp
import numpy as np
from jax import lax
from jax.experimental import pallas as pl
from jax.experimental.pallas import tpu as pltpu
from jax.sharding import PartitionSpec as P

ITERS = 4
GROUPS = (3,)
VMEM_LIMIT = 24 * 2**20

learn_rate = 0.1
beta_one = 0.9
beta_two = 0.999
adam_eps = 1e-08
first_step = 10
resist_gain = 3.0
resist_level = 1.0

BF = jnp.bfloat16
F32 = jnp.float32


def dot(left, right):
    return jnp.dot(left, right, preferred_element_type=F32)


def cos_sin(band, pixels, places):
    freq = np.arange(band, dtype=np.int64) - band // 2
    phase = (freq[None, :] * np.asarray(places, np.int64)[:, None]) % pixels
    angle = phase * (2.0 * np.pi / pixels)
    return np.concatenate([np.cos(angle), np.sin(angle)], axis=1)


def interpolation(coarse, pixels):
    step = pixels // coarse
    offset = (np.arange(pixels)[:, None] - step * np.arange(coarse)[None, :]) % pixels
    freq = np.arange(1, coarse // 2)
    kernel = 1.0 + 2.0 * np.cos(
        2.0 * np.pi * ((freq[None, :] * np.arange(pixels)[:, None]) % pixels) / pixels
    ).sum(axis=1)
    return kernel[offset] / coarse


def for_each(count, step):
    if count == 1:
        step(0)
    else:
        lax.fori_loop(0, count, lambda i, c: (step(i), c)[1], 0)


def call(body, out_shape, args, scratch=(), flops=0, scalars=(), limit=VMEM_LIMIT):
    vmem = pl.BlockSpec(memory_space=pltpu.VMEM)
    smem = pl.BlockSpec(memory_space=pltpu.SMEM)
    many = isinstance(out_shape, (list, tuple))
    nbytes = sum(int(np.prod(a.shape)) * a.dtype.itemsize for a in args)
    return pl.pallas_call(
        body,
        out_shape=out_shape,
        in_specs=[smem] * len(scalars) + [vmem] * len(args),
        out_specs=[vmem] * len(out_shape) if many else vmem,
        scratch_shapes=list(scratch),
        compiler_params=pltpu.CompilerParams(vmem_limit_bytes=limit),
        cost_estimate=pl.CostEstimate(flops=flops, bytes_accessed=nbytes, transcendentals=0),
    )(*scalars, *args)


def square(real, imag):
    return jnp.concatenate(
        [jnp.concatenate([real, imag], axis=1), jnp.concatenate([-imag, real], axis=1)], axis=0
    )


def unpack_kernel(words_ref, picks_ref, shift_ref, sign_ref):
    def image(i):
        words = words_ref[i]
        value = None
        for q in range(4):
            byte = (jnp.right_shift(words, 8 * q) & 255).astype(F32).astype(BF)
            part = dot(byte, picks_ref[q])
            value = part if value is None else value + part
        bits = jnp.right_shift(value.astype(jnp.int32), shift_ref[...]) & 1
        sign_ref[i] = (1 - 2 * bits).astype(F32).astype(BF)

    for_each(sign_ref.shape[0], image)


def spectrum_part(core, theta, across_y, down_x, band, pixels):
    mask_bf = jnp.tanh(theta).astype(BF)
    across = dot(mask_bf, across_y).astype(BF)
    part = dot(down_x, across) * (1.0 / pixels)
    real = part[:band, :band] - part[band:, band:]
    imag = -(part[band:, :band] + part[:band, band:])
    first = core == 0
    return jnp.where(first, real, imag).astype(BF), jnp.where(first, imag, real).astype(BF)


def mask_kernel(band, pixels, core_ref, theta_ref, across_y_ref, down_x_ref, mine_ref, theirs_ref):
    for i in range(theta_ref.shape[0]):
        mine_ref[i], theirs_ref[i] = spectrum_part(
            core_ref[0], theta_ref[i], across_y_ref[...], down_x_ref[...], band, pixels
        )


def update_kernel(
    band,
    pixels,
    step_number,
    last,
    core_ref,
    adjoint_ref,
    other_ref,
    theta_ref,
    first_ref,
    second_ref,
    along_x_ref,
    onto_y_ref,
    across_y_ref,
    down_x_ref,
    new_theta_ref,
    new_first_ref,
    new_second_ref,
    *out_refs,
):
    fix_one = 1.0 - beta_one**step_number
    fix_two = 1.0 - beta_two**step_number
    for i in range(theta_ref.shape[0]):
        real = (adjoint_ref[0, i].astype(F32) + other_ref[0, i].astype(F32)).astype(BF)
        imag = (adjoint_ref[1, i].astype(F32) + other_ref[1, i].astype(F32)).astype(BF)
        rows = dot(along_x_ref[...], square(real, imag)).astype(BF)
        mask_grad = dot(rows, onto_y_ref[...]) * (1.0 / pixels)
        theta = theta_ref[i]
        gradient = mask_grad * (1.0 - jnp.tanh(theta) ** 2)
        new_first = beta_one * first_ref[i] + (1.0 - beta_one) * gradient
        new_second = beta_two * second_ref[i] + (1.0 - beta_two) * gradient * gradient
        new_theta = theta - learn_rate * (new_first / fix_one) / (
            jnp.sqrt(new_second / fix_two) + adam_eps
        )
        new_theta_ref[i] = new_theta
        new_first_ref[i] = new_first
        new_second_ref[i] = new_second
        if last:
            out_refs[0][i] = gradient
        else:
            out_refs[0][i], out_refs[1][i] = spectrum_part(
                core_ref[0], new_theta, across_y_ref[...], down_x_ref[...], band, pixels
            )


def field_kernel(
    core_ref,
    mine_ref,
    other_ref,
    kernels_ref,
    rows_ref,
    columns_ref,
    fields_ref,
    intensity_ref,
    half_ref,
):
    kernel_count = kernels_ref.shape[1]
    coarse = rows_ref.shape[0]
    first = core_ref[0] == 0

    def image(i):
        mine = mine_ref[i].astype(F32)
        other = other_ref[i].astype(F32)
        spectrum_real = jnp.where(first, mine, other)
        spectrum_imag = jnp.where(first, other, mine)
        for k in range(kernel_count):
            kernel_real = kernels_ref[0, k].astype(F32)
            kernel_imag = kernels_ref[1, k].astype(F32)
            real = (kernel_real * spectrum_real - kernel_imag * spectrum_imag).astype(BF)
            imag = (kernel_real * spectrum_imag + kernel_imag * spectrum_real).astype(BF)
            half_ref[k] = dot(rows_ref[...], square(real, imag)).astype(BF)
        total = None
        for k in range(kernel_count):
            field = dot(half_ref[k], columns_ref[...])
            fields_ref[i, k] = field.astype(BF)
            field_real, field_imag = field[:, :coarse], field[:, coarse:]
            power = field_real * field_real + field_imag * field_imag
            total = power if total is None else total + power
        intensity_ref[i] = total.astype(BF)

    for_each(fields_ref.shape[0], image)


def resist_kernel(
    own_ref, other_ref, sign_ref, up_x_ref, down_x_ref, up_y_ref, down_y_ref, out_ref, drive_ref
):
    pixels, coarse = up_x_ref.shape
    chunk = min(256, pixels)
    half_gain = 0.5 * resist_gain

    def image(i):
        intensity = (own_ref[i].astype(F32) + other_ref[i].astype(F32)).astype(BF)
        wide = dot(intensity, up_y_ref[...]).astype(BF)
        for start in range(0, pixels, chunk):
            fine = dot(up_x_ref[start : start + chunk, :], wide)
            bent = jnp.tanh(half_gain * fine - half_gain * resist_level)
            sign = sign_ref[i, start : start + chunk, :].astype(F32)
            drive = (bent + sign) * (1.0 - bent * bent)
            drive_ref[start : start + chunk, :] = drive.astype(BF)
        total = dot(down_x_ref[...], drive_ref[...])
        out_ref[i] = dot(total.astype(BF), down_y_ref[...]).astype(BF)

    for_each(own_ref.shape[0], image)


def adjoint_kernel(
    own_ref, other_ref, fields_ref, kernels_ref, columns_ref, rows_ref, out_ref, back_ref
):
    kernel_count = kernels_ref.shape[1]
    band = kernels_ref.shape[3]

    def image(i):
        drive = (own_ref[i].astype(F32) + other_ref[i].astype(F32)).astype(BF)
        drive_twice = jnp.concatenate([drive, drive], axis=1)
        for k in range(kernel_count):
            push = drive_twice * fields_ref[i, k]
            back_ref[k] = dot(push, columns_ref[...]).astype(BF)
        total_real = total_imag = None
        for k in range(kernel_count):
            parts = dot(rows_ref[...], back_ref[k])
            spectral_real = parts[:band, :band] + parts[band:, band:]
            spectral_imag = parts[:band, band:] - parts[band:, :band]
            kernel_real = kernels_ref[0, k].astype(F32)
            kernel_imag = kernels_ref[1, k].astype(F32)
            term_real = kernel_real * spectral_real + kernel_imag * spectral_imag
            term_imag = kernel_real * spectral_imag - kernel_imag * spectral_real
            total_real = term_real if total_real is None else total_real + term_real
            total_imag = term_imag if total_imag is None else total_imag + term_imag
        scale = 0.25 * resist_gain
        out_ref[0, i] = (scale * total_real).astype(BF)
        out_ref[1, i] = (scale * total_imag).astype(BF)

    for_each(own_ref.shape[0], image)


def swap(value, axis, mask):
    count = lax.axis_size(axis)
    return lax.ppermute(value, axis, [(i, i ^ mask) for i in range(count)])


def add(first, *others):
    total = first.astype(F32)
    for other in others:
        total = total + other.astype(F32)
    return total.astype(BF)


def sum_axis(value, axis, unit, count):
    if count <= 4:
        return add(value, *[swap(value, axis, unit * m) for m in range(1, count)])
    bit = 1
    while bit < count:
        value = add(value, swap(value, axis, unit * bit))
        bit *= 2
    return value


def in_order(blocks, at):
    count = len(blocks)
    return jnp.take(jnp.stack(blocks), jnp.arange(count, dtype=jnp.int32) ^ at, axis=0)


def body(mask_theta, first_moment, second_moment, target_bits, kernels, kernel_weights):
    tile_count, row_count, column_count = mask_theta.shape
    word_count = target_bits.shape[2]
    band = kernels.shape[-1]
    coarse = 2 * band
    tiles = lax.axis_size("tile")
    chips = lax.axis_size("kern") // 2
    pixels = tiles * row_count
    strip = chips * column_count
    step = pixels // coarse
    tile_at = lax.axis_index("tile")
    kern_at = lax.axis_index("kern")
    core = kern_at % 2
    core_scalar = core.astype(jnp.int32).reshape(1)

    fine = cos_sin(band, pixels, np.arange(pixels))
    fine_table = jnp.asarray(fine, BF)
    fine_table_t = jnp.asarray(fine.T, BF)
    signed_t = jnp.asarray(np.concatenate([fine.T[:band], -fine.T[band:]]), BF)
    up = interpolation(coarse, pixels)
    up_table = jnp.asarray(up, BF)
    up_table_t = jnp.asarray(up.T, BF)
    coarse_rows = fine[::step]
    cos_c, sin_c = coarse_rows[:, :band], coarse_rows[:, band:]
    field_rows = jnp.asarray(coarse_rows, BF)
    field_columns = jnp.asarray(
        np.block([[cos_c.T, sin_c.T], [-sin_c.T, cos_c.T]]) / band, BF
    )
    back_columns = jnp.asarray(np.block([[cos_c, -sin_c], [sin_c, cos_c]]) * (2.0 / band), BF)
    back_rows = jnp.asarray(coarse_rows.T, BF)
    place = np.arange(strip) % column_count
    word_of = (np.arange(strip) // column_count) * word_count + place // 30
    bit_of = place % 30
    picks = jnp.asarray(
        (np.arange(chips * word_count)[None, :, None] == word_of)
        & (np.arange(4)[:, None, None] == bit_of // 8),
        BF,
    )
    shift = jnp.asarray((bit_of % 8)[None, :], jnp.int32)

    row_start = tile_at * row_count
    column_start = kern_at * column_count
    along_x = lax.dynamic_slice_in_dim(fine_table, row_start, row_count, 0)
    down_x = lax.dynamic_slice_in_dim(fine_table_t, row_start, row_count, 1)
    across_y = lax.dynamic_slice_in_dim(fine_table, column_start, column_count, 0)
    onto_y = lax.dynamic_slice_in_dim(signed_t, column_start, column_count, 1)

    groups, start = [], 0
    for size in GROUPS:
        groups.append(slice(start, start + size))
        start += size

    def spread(shape, dtype=BF):
        return jax.ShapeDtypeStruct(shape, dtype)

    def sum_all(mine, theirs):
        mine = add(mine, swap(theirs, "kern", 1))
        mine = sum_axis(mine, "kern", 2, chips)
        mine = sum_axis(mine, "tile", 1, tiles)
        return mine, swap(mine, "kern", 1)

    parts = []
    for group in groups:
        count = group.stop - group.start
        parts.append(
            call(
                functools.partial(mask_kernel, band, pixels),
                [spread((count, band, band))] * 2,
                (mask_theta[group], across_y, down_x),
                scalars=(core_scalar,),
                flops=count * 10**8,
            )
        )

    kernels, target_bits, _ = lax.optimization_barrier((kernels, target_bits, parts))
    scaled = (kernels * jnp.sqrt(kernel_weights)[None, :, None, None]).astype(BF)
    own_kernels = jnp.concatenate(
        [scaled] + [swap(scaled, "kern", 2 * m) for m in range(1, chips)], axis=1
    )
    words = in_order([target_bits] + [swap(target_bits, "tile", m) for m in range(1, tiles)], tile_at)
    words = jnp.moveaxis(words, 0, 1).reshape(tile_count, pixels, word_count)
    words = jnp.concatenate(
        [words] + [swap(words, "kern", 2 * m) for m in range(1, chips)], axis=2
    )
    starts = [(kern_at ^ (2 * m)) * column_count for m in range(chips)]
    up_y = jnp.concatenate(
        [lax.dynamic_slice_in_dim(up_table_t, at, column_count, 1) for at in starts], axis=1
    )
    down_y = jnp.concatenate(
        [lax.dynamic_slice_in_dim(up_table, at, column_count, 0) for at in starts], axis=0
    )

    results = []
    for group, (mine, theirs) in zip(groups, parts):
        count = group.stop - group.start
        theta, first, second = mask_theta[group], first_moment[group], second_moment[group]
        block = spread(theta.shape, F32)
        sign = call(
            unpack_kernel,
            spread((count, pixels, strip)),
            (words[group], picks, shift),
            flops=count * 2 * 10**8,
        )
        gradient = None
        for iteration in range(ITERS):
            mine, other = sum_all(mine, theirs)
            kernel_count = own_kernels.shape[1]
            fields, intensity = call(
                field_kernel,
                [
                    spread((count, kernel_count, coarse, 2 * coarse)),
                    spread((count, coarse, coarse)),
                ],
                (mine, other, own_kernels, field_rows, field_columns),
                scalars=(core_scalar,),
                scratch=[pltpu.VMEM((kernel_count, coarse, coarse), BF)],
                flops=count * 10**9,
            )
            drive = call(
                resist_kernel,
                spread((count, coarse, coarse)),
                (intensity, swap(intensity, "kern", 1), sign, up_table, up_table_t, up_y, down_y),
                scratch=[pltpu.VMEM((pixels, strip), BF)],
                flops=count * 7 * 10**8,
            )
            adjoint = call(
                adjoint_kernel,
                spread((2, count, band, band)),
                (drive, swap(drive, "kern", 1), fields, own_kernels, back_columns, back_rows),
                scratch=[pltpu.VMEM((kernel_count, coarse, coarse), BF)],
                flops=count * 10**9,
            )
            last = iteration == ITERS - 1
            theta, first, second, *out = call(
                functools.partial(update_kernel, band, pixels, first_step + iteration, last),
                [block] * 3 + ([block] if last else [spread((count, band, band))] * 2),
                (
                    adjoint,
                    swap(adjoint, "kern", 1),
                    theta,
                    first,
                    second,
                    along_x,
                    onto_y,
                    across_y,
                    down_x,
                ),
                scalars=(core_scalar,),
                flops=count * 2 * 10**8,
            )
            if last:
                gradient = out[0]
            else:
                mine, theirs = out
        results.append((theta, first, second, gradient))
    return tuple(jnp.concatenate(parts) if len(parts) > 1 else parts[0] for parts in zip(*results))


def solution(mesh):
    block = P("grp", "tile", "kern")
    return jax.shard_map(
        body,
        mesh=mesh,
        in_specs=(block, block, block, block, P(None, "kern", None, None), P("kern")),
        out_specs=(block, block, block, block),
        check_vma=False,
    )
```

```python
import functools

import jax
import jax.numpy as jnp
import numpy as np
from jax import lax
from jax.experimental import pallas as pl
from jax.experimental.pallas import tpu as pltpu
from jax.sharding import PartitionSpec as P

ITERS = 4
BATCHES = ((0, 1, 2),)
VMEM_LIMIT = 24 * 2**20

learn_rate = 0.1
beta_one = 0.9
beta_two = 0.999
adam_eps = 1e-08
first_step = 10
resist_gain = 3.0
resist_level = 1.0

BF = jnp.bfloat16
F32 = jnp.float32


def dot(left, right):
    return jnp.dot(left, right, preferred_element_type=F32)


def cos_sin(band, pixels, places):
    freq = np.arange(band, dtype=np.int64) - band // 2
    phase = (freq[None, :] * np.asarray(places, np.int64)[:, None]) % pixels
    angle = phase * (2.0 * np.pi / pixels)
    return np.concatenate([np.cos(angle), np.sin(angle)], axis=1)


def interpolation(coarse, pixels):
    step = pixels // coarse
    offset = (np.arange(pixels)[:, None] - step * np.arange(coarse)[None, :]) % pixels
    freq = np.arange(1, coarse // 2)
    kernel = 1.0 + 2.0 * np.cos(
        2.0 * np.pi * ((freq[None, :] * np.arange(pixels)[:, None]) % pixels) / pixels
    ).sum(axis=1)
    return kernel[offset] / coarse


def for_each(count, step):
    if count == 1:
        step(0)
    else:
        lax.fori_loop(0, count, lambda i, c: (step(i), c)[1], 0)


def call(body, out_shape, args, scratch=(), flops=0, scalars=(), limit=VMEM_LIMIT):
    vmem = pl.BlockSpec(memory_space=pltpu.VMEM)
    smem = pl.BlockSpec(memory_space=pltpu.SMEM)
    many = isinstance(out_shape, (list, tuple))
    nbytes = sum(int(np.prod(a.shape)) * a.dtype.itemsize for a in args)
    return pl.pallas_call(
        body,
        out_shape=out_shape,
        in_specs=[smem] * len(scalars) + [vmem] * len(args),
        out_specs=[vmem] * len(out_shape) if many else vmem,
        scratch_shapes=list(scratch),
        compiler_params=pltpu.CompilerParams(vmem_limit_bytes=limit),
        cost_estimate=pl.CostEstimate(flops=flops, bytes_accessed=nbytes, transcendentals=0),
    )(*scalars, *args)


def square(real, imag):
    return jnp.concatenate(
        [jnp.concatenate([real, imag], axis=1), jnp.concatenate([-imag, real], axis=1)], axis=0
    )


def unpack_kernel(image, at_ref, *refs):
    *pieces, picks_ref, shift_ref, sign_ref = refs
    rows = pieces[0].shape[-1]
    for m, piece in enumerate(pieces):
        words = jnp.concatenate([piece[c, image] for c in range(piece.shape[0])], axis=0)
        parts = [jnp.right_shift(words, 8 * q) & 255 for q in range(4)]
        octets = jnp.concatenate(parts, axis=0).astype(F32).astype(BF)
        value = lax.dot_general(
            octets, picks_ref[...], (((0,), (0,)), ((), ())), preferred_element_type=F32
        )
        bits = jnp.right_shift(value.astype(jnp.int32), shift_ref[...]) & 1
        start = pl.multiple_of((at_ref[0] ^ m) * rows, rows)
        sign_ref[pl.ds(start, rows), :] = (1 - 2 * bits).astype(F32).astype(BF)


def spectrum_part(core, theta, across_y, down_x, band, pixels):
    mask_bf = jnp.tanh(theta).astype(BF)
    across = dot(mask_bf, across_y).astype(BF)
    part = dot(down_x, across) * (1.0 / pixels)
    real = part[:band, :band] - part[band:, band:]
    imag = -(part[band:, :band] + part[:band, band:])
    first = core == 0
    return jnp.where(first, real, imag).astype(BF), jnp.where(first, imag, real).astype(BF)


def mask_kernel(band, pixels, core_ref, theta_ref, across_y_ref, down_x_ref, mine_ref, theirs_ref):
    for i in range(theta_ref.shape[0]):
        mine_ref[i], theirs_ref[i] = spectrum_part(
            core_ref[0], theta_ref[i], across_y_ref[...], down_x_ref[...], band, pixels
        )


def update_kernel(
    band,
    pixels,
    step_number,
    last,
    core_ref,
    adjoint_ref,
    other_ref,
    theta_ref,
    first_ref,
    second_ref,
    along_x_ref,
    onto_y_ref,
    across_y_ref,
    down_x_ref,
    new_theta_ref,
    new_first_ref,
    new_second_ref,
    *out_refs,
):
    fix_one = 1.0 - beta_one**step_number
    fix_two = 1.0 - beta_two**step_number
    for i in range(theta_ref.shape[0]):
        real = (adjoint_ref[0, i].astype(F32) + other_ref[0, i].astype(F32)).astype(BF)
        imag = (adjoint_ref[1, i].astype(F32) + other_ref[1, i].astype(F32)).astype(BF)
        rows = dot(along_x_ref[...], square(real, imag)).astype(BF)
        mask_grad = dot(rows, onto_y_ref[...]) * (1.0 / pixels)
        theta = theta_ref[i]
        gradient = mask_grad * (1.0 - jnp.tanh(theta) ** 2)
        new_first = beta_one * first_ref[i] + (1.0 - beta_one) * gradient
        new_second = beta_two * second_ref[i] + (1.0 - beta_two) * gradient * gradient
        new_theta = theta - learn_rate * (new_first / fix_one) / (
            jnp.sqrt(new_second / fix_two) + adam_eps
        )
        new_theta_ref[i] = new_theta
        new_first_ref[i] = new_first
        new_second_ref[i] = new_second
        if last:
            out_refs[0][i] = gradient
        else:
            out_refs[0][i], out_refs[1][i] = spectrum_part(
                core_ref[0], new_theta, across_y_ref[...], down_x_ref[...], band, pixels
            )


def field_kernel(
    core_ref,
    mine_ref,
    other_ref,
    kernels_ref,
    rows_ref,
    columns_ref,
    fields_ref,
    intensity_ref,
    half_ref,
):
    kernel_count = kernels_ref.shape[1]
    coarse = rows_ref.shape[0]
    first = core_ref[0] == 0

    def image(i):
        mine = mine_ref[i].astype(F32)
        other = other_ref[i].astype(F32)
        spectrum_real = jnp.where(first, mine, other)
        spectrum_imag = jnp.where(first, other, mine)
        for k in range(kernel_count):
            kernel_real = kernels_ref[0, k].astype(F32)
            kernel_imag = kernels_ref[1, k].astype(F32)
            real = (kernel_real * spectrum_real - kernel_imag * spectrum_imag).astype(BF)
            imag = (kernel_real * spectrum_imag + kernel_imag * spectrum_real).astype(BF)
            half_ref[k] = dot(rows_ref[...], square(real, imag)).astype(BF)
        total = None
        for k in range(kernel_count):
            field = dot(half_ref[k], columns_ref[...])
            fields_ref[i, k] = field.astype(BF)
            field_real, field_imag = field[:, :coarse], field[:, coarse:]
            power = field_real * field_real + field_imag * field_imag
            total = power if total is None else total + power
        intensity_ref[i] = total.astype(BF)

    for_each(fields_ref.shape[0], image)


def resist_kernel(
    own_ref, other_ref, sign_ref, up_x_ref, down_x_ref, up_y_ref, down_y_ref, out_ref, drive_ref
):
    pixels, coarse = up_x_ref.shape
    chunk = min(256, pixels)
    half_gain = 0.5 * resist_gain

    def image(i):
        intensity = (own_ref[i].astype(F32) + other_ref[i].astype(F32)).astype(BF)
        wide = dot(intensity, up_y_ref[...]).astype(BF)
        for start in range(0, pixels, chunk):
            fine = dot(up_x_ref[start : start + chunk, :], wide)
            bent = jnp.tanh(half_gain * fine - half_gain * resist_level)
            sign = sign_ref[start : start + chunk, :].astype(F32)
            drive = (bent + sign) * (1.0 - bent * bent)
            drive_ref[start : start + chunk, :] = drive.astype(BF)
        total = dot(down_x_ref[...], drive_ref[...])
        out_ref[i] = dot(total.astype(BF), down_y_ref[...]).astype(BF)

    for_each(own_ref.shape[0], image)


def adjoint_kernel(
    own_ref, other_ref, fields_ref, kernels_ref, columns_ref, rows_ref, out_ref, back_ref
):
    kernel_count = kernels_ref.shape[1]
    band = kernels_ref.shape[3]

    def image(i):
        drive = (own_ref[i].astype(F32) + other_ref[i].astype(F32)).astype(BF)
        drive_twice = jnp.concatenate([drive, drive], axis=1)
        for k in range(kernel_count):
            push = drive_twice * fields_ref[i, k]
            back_ref[k] = dot(push, columns_ref[...]).astype(BF)
        total_real = total_imag = None
        for k in range(kernel_count):
            parts = dot(rows_ref[...], back_ref[k])
            spectral_real = parts[:band, :band] + parts[band:, band:]
            spectral_imag = parts[:band, band:] - parts[band:, :band]
            kernel_real = kernels_ref[0, k].astype(F32)
            kernel_imag = kernels_ref[1, k].astype(F32)
            term_real = kernel_real * spectral_real + kernel_imag * spectral_imag
            term_imag = kernel_real * spectral_imag - kernel_imag * spectral_real
            total_real = term_real if total_real is None else total_real + term_real
            total_imag = term_imag if total_imag is None else total_imag + term_imag
        scale = 0.25 * resist_gain
        out_ref[0, i] = (scale * total_real).astype(BF)
        out_ref[1, i] = (scale * total_imag).astype(BF)

    for_each(own_ref.shape[0], image)


def swap(value, axis, mask):
    count = lax.axis_size(axis)
    return lax.ppermute(value, axis, [(i, i ^ mask) for i in range(count)])


def add(first, *others):
    total = first.astype(F32)
    for other in others:
        total = total + other.astype(F32)
    return total.astype(BF)


def sum_axis(value, axis, unit, count):
    if count <= 4:
        return add(value, *[swap(value, axis, unit * m) for m in range(1, count)])
    bit = 1
    while bit < count:
        value = add(value, swap(value, axis, unit * bit))
        bit *= 2
    return value


def body(mask_theta, first_moment, second_moment, target_bits, kernels, kernel_weights):
    tile_count, row_count, column_count = mask_theta.shape
    word_count = target_bits.shape[2]
    band = kernels.shape[-1]
    coarse = 2 * band
    tiles = lax.axis_size("tile")
    chips = lax.axis_size("kern") // 2
    pixels = tiles * row_count
    strip = chips * column_count
    step = pixels // coarse
    tile_at = lax.axis_index("tile")
    kern_at = lax.axis_index("kern")
    core = kern_at % 2
    core_scalar = core.astype(jnp.int32).reshape(1)

    fine = cos_sin(band, pixels, np.arange(pixels))
    fine_table = jnp.asarray(fine, BF)
    fine_table_t = jnp.asarray(fine.T, BF)
    signed_t = jnp.asarray(np.concatenate([fine.T[:band], -fine.T[band:]]), BF)
    up = interpolation(coarse, pixels)
    up_table = jnp.asarray(up, BF)
    up_table_t = jnp.asarray(up.T, BF)
    coarse_rows = fine[::step]
    cos_c, sin_c = coarse_rows[:, :band], coarse_rows[:, band:]
    field_rows = jnp.asarray(coarse_rows, BF)
    field_columns = jnp.asarray(
        np.block([[cos_c.T, sin_c.T], [-sin_c.T, cos_c.T]]) / band, BF
    )
    back_columns = jnp.asarray(np.block([[cos_c, -sin_c], [sin_c, cos_c]]) * (2.0 / band), BF)
    back_rows = jnp.asarray(coarse_rows.T, BF)
    place = np.arange(strip) % column_count
    padded = -(-word_count // 8) * 8
    word_of = (np.arange(strip) // column_count) * padded + place // 30
    bit_of = place % 30
    picks = jnp.asarray(
        (
            (np.arange(chips * padded)[None, :, None] == word_of)
            & (np.arange(4)[:, None, None] == bit_of // 8)
        ).reshape(4 * chips * padded, strip),
        BF,
    )
    shift = jnp.asarray((bit_of % 8)[None, :], jnp.int32)

    row_start = tile_at * row_count
    column_start = kern_at * column_count
    along_x = lax.dynamic_slice_in_dim(fine_table, row_start, row_count, 0)
    down_x = lax.dynamic_slice_in_dim(fine_table_t, row_start, row_count, 1)
    across_y = lax.dynamic_slice_in_dim(fine_table, column_start, column_count, 0)
    onto_y = lax.dynamic_slice_in_dim(signed_t, column_start, column_count, 1)

    def spread(shape, dtype=BF):
        return jax.ShapeDtypeStruct(shape, dtype)

    def after(values, anchor):
        return lax.optimization_barrier((values, anchor))[0]

    half = spread((1, band, band))
    block = spread((1, row_count, column_count), F32)
    states = [
        (mask_theta[i : i + 1], first_moment[i : i + 1], second_moment[i : i + 1])
        for i in range(tile_count)
    ]
    mine, theirs = call(
        functools.partial(mask_kernel, band, pixels),
        [spread((tile_count, band, band))] * 2,
        (mask_theta, across_y, down_x),
        scalars=(core_scalar,),
        flops=tile_count * 10**8,
    )
    mine = add(mine, swap(theirs, "kern", 1))

    scaled = (after(kernels, mine) * jnp.sqrt(kernel_weights)[None, :, None, None]).astype(BF)
    words = jnp.pad(
        jnp.swapaxes(after(target_bits, mine), 1, 2), ((0, 0), (0, padded - word_count), (0, 0))
    )
    mine = sum_axis(mine, "kern", 2, chips)
    words = jnp.stack([words] + [swap(words, "kern", 2 * m) for m in range(1, chips)])
    own_kernels = jnp.concatenate(
        [scaled] + [swap(scaled, "kern", 2 * m) for m in range(1, chips)], axis=1
    )
    kernel_count = own_kernels.shape[1]
    words = after(words, mine)
    mine = sum_axis(mine, "tile", 1, tiles)
    pieces = [words] + [swap(words, "tile", m) for m in range(1, tiles)]
    trade = swap(mine, "kern", 1)
    spectra = [(mine[i : i + 1], trade[i : i + 1]) for i in range(tile_count)]

    starts = [(kern_at ^ (2 * m)) * column_count for m in range(chips)]
    up_y = jnp.concatenate(
        [lax.dynamic_slice_in_dim(up_table_t, at, column_count, 1) for at in starts], axis=1
    )
    down_y = jnp.concatenate(
        [lax.dynamic_slice_in_dim(up_table, at, column_count, 0) for at in starts], axis=0
    )
    signs = [
        call(
            functools.partial(unpack_kernel, i),
            spread((pixels, strip)),
            (*pieces, picks, shift),
            scalars=(tile_at.astype(jnp.int32).reshape(1),),
            flops=2 * 10**8,
        )
        for i in range(tile_count)
    ]

    gradients = [None] * tile_count
    for iteration in range(ITERS):
        last = iteration == ITERS - 1
        parts = [None] * tile_count
        for i in range(tile_count):
            fields, intensity = call(
                field_kernel,
                [
                    spread((1, kernel_count, coarse, 2 * coarse)),
                    spread((1, coarse, coarse)),
                ],
                (*spectra[i], own_kernels, field_rows, field_columns),
                scalars=(core_scalar,),
                scratch=[pltpu.VMEM((kernel_count, coarse, coarse), BF)],
                flops=10**9,
            )
            drive = call(
                resist_kernel,
                spread((1, coarse, coarse)),
                (
                    intensity,
                    swap(intensity, "kern", 1),
                    signs[i],
                    up_table,
                    up_table_t,
                    up_y,
                    down_y,
                ),
                scratch=[pltpu.VMEM((pixels, strip), BF)],
                flops=7 * 10**8,
            )
            adjoint = call(
                adjoint_kernel,
                spread((2, 1, band, band)),
                (drive, swap(drive, "kern", 1), fields, own_kernels, back_columns, back_rows),
                scratch=[pltpu.VMEM((kernel_count, coarse, coarse), BF)],
                flops=10**9,
            )
            theta, first, second, *out = call(
                functools.partial(update_kernel, band, pixels, first_step + iteration, last),
                [block] * 3 + ([block] if last else [half] * 2),
                (
                    adjoint,
                    swap(adjoint, "kern", 1),
                    *states[i],
                    along_x,
                    onto_y,
                    across_y,
                    down_x,
                ),
                scalars=(core_scalar,),
                flops=2 * 10**8,
            )
            states[i] = (theta, first, second)
            if last:
                gradients[i] = out[0]
            else:
                parts[i] = add(out[0], swap(out[1], "kern", 1))
        if last:
            break
        for batch in BATCHES:
            mine = jnp.concatenate([parts[i] for i in batch])
            mine = sum_axis(mine, "kern", 2, chips)
            mine = sum_axis(mine, "tile", 1, tiles)
            trade = swap(mine, "kern", 1)
            for at, i in enumerate(batch):
                spectra[i] = (mine[at : at + 1], trade[at : at + 1])
    outs = [jnp.concatenate([state[j] for state in states]) for j in range(3)]
    return (*outs, jnp.concatenate(gradients))


def solution(mesh):
    block = P("grp", "tile", "kern")
    return jax.shard_map(
        body,
        mesh=mesh,
        in_specs=(block, block, block, block, P(None, "kern", None, None), P("kern")),
        out_specs=(block, block, block, block),
        check_vma=False,
    )
```

```python
import functools

import jax
import jax.numpy as jnp
import numpy as np
from jax import lax
from jax.experimental import pallas as pl
from jax.experimental.pallas import tpu as pltpu
from jax.sharding import PartitionSpec as P

ITERS = 4
PAIRED = True
GROUPS = ((0, 1, 2),)
VMEM_LIMIT = 24 * 2**20

learn_rate = 0.1
beta_one = 0.9
beta_two = 0.999
adam_eps = 1e-08
first_step = 10
resist_gain = 3.0
resist_level = 1.0

BF = jnp.bfloat16
F32 = jnp.float32


def dot(left, right):
    return jnp.dot(left, right, preferred_element_type=F32)


def cos_sin(band, pixels, places):
    freq = np.arange(band, dtype=np.int64) - band // 2
    phase = (freq[None, :] * np.asarray(places, np.int64)[:, None]) % pixels
    angle = phase * (2.0 * np.pi / pixels)
    return np.concatenate([np.cos(angle), np.sin(angle)], axis=1)


def interpolation(coarse, pixels):
    step = pixels // coarse
    offset = (np.arange(pixels)[:, None] - step * np.arange(coarse)[None, :]) % pixels
    freq = np.arange(1, coarse // 2)
    kernel = 1.0 + 2.0 * np.cos(
        2.0 * np.pi * ((freq[None, :] * np.arange(pixels)[:, None]) % pixels) / pixels
    ).sum(axis=1)
    return kernel[offset] / coarse


def for_each(count, step):
    if count == 1:
        step(0)
    else:
        lax.fori_loop(0, count, lambda i, c: (step(i), c)[1], 0)


def call(body, out_shape, args, scratch=(), flops=0, scalars=(), limit=VMEM_LIMIT):
    vmem = pl.BlockSpec(memory_space=pltpu.VMEM)
    smem = pl.BlockSpec(memory_space=pltpu.SMEM)
    many = isinstance(out_shape, (list, tuple))
    nbytes = sum(int(np.prod(a.shape)) * a.dtype.itemsize for a in args)
    return pl.pallas_call(
        body,
        out_shape=out_shape,
        in_specs=[smem] * len(scalars) + [vmem] * len(args),
        out_specs=[vmem] * len(out_shape) if many else vmem,
        scratch_shapes=list(scratch),
        compiler_params=pltpu.CompilerParams(vmem_limit_bytes=limit),
        cost_estimate=pl.CostEstimate(flops=flops, bytes_accessed=nbytes, transcendentals=0),
    )(*scalars, *args)


def square(real, imag):
    return jnp.concatenate(
        [jnp.concatenate([real, imag], axis=1), jnp.concatenate([-imag, real], axis=1)], axis=0
    )


def unpack_kernel(at_ref, image_ref, pieces_ref, picks_ref, shift_ref, sign_ref):
    chips, tiles, _, _, rows = pieces_ref.shape
    image = image_ref[0]
    for m in range(tiles):
        words = jnp.concatenate([pieces_ref[c, m, image] for c in range(chips)], axis=0)
        parts = [jnp.right_shift(words, 8 * q) & 255 for q in range(4)]
        octets = jnp.concatenate(parts, axis=0).astype(F32).astype(BF)
        value = lax.dot_general(
            octets, picks_ref[...], (((0,), (0,)), ((), ())), preferred_element_type=F32
        )
        bits = jnp.right_shift(value.astype(jnp.int32), shift_ref[...]) & 1
        start = pl.multiple_of((at_ref[0] ^ m) * rows, rows)
        sign_ref[pl.ds(start, rows), :] = (1 - 2 * bits).astype(F32).astype(BF)


def spectrum_part(core, theta, across_y, down_x, band, pixels):
    mask_bf = jnp.tanh(theta).astype(BF)
    across = dot(mask_bf, across_y).astype(BF)
    part = dot(down_x, across) * (1.0 / pixels)
    real = part[:band, :band] - part[band:, band:]
    imag = -(part[band:, :band] + part[:band, band:])
    first = core == 0
    return jnp.where(first, real, imag).astype(BF), jnp.where(first, imag, real).astype(BF)


def mask_kernel(band, pixels, core_ref, theta_ref, across_y_ref, down_x_ref, mine_ref, theirs_ref):
    for i in range(theta_ref.shape[0]):
        mine_ref[i], theirs_ref[i] = spectrum_part(
            core_ref[0], theta_ref[i], across_y_ref[...], down_x_ref[...], band, pixels
        )


def update_kernel(band, pixels, last, core_ref, fix_ref, *refs):
    split = len(refs) - 8 - (1 if last else 2)
    *adjoint_refs, theta_ref, first_ref, second_ref = refs[:split + 1]
    along_x_ref, onto_y_ref, across_y_ref, down_x_ref = refs[split + 1 : split + 5]
    new_theta_ref, new_first_ref, new_second_ref, *out_refs = refs[split + 5 :]
    pairs = []
    for own_ref, other_ref in zip(adjoint_refs[::2], adjoint_refs[1::2]):
        pairs += [(own_ref, other_ref, at) for at in range(own_ref.shape[1])]
    for i, (own_ref, other_ref, at) in enumerate(pairs):
        real = (own_ref[0, at].astype(F32) + other_ref[0, at].astype(F32)).astype(BF)
        imag = (own_ref[1, at].astype(F32) + other_ref[1, at].astype(F32)).astype(BF)
        rows = dot(along_x_ref[...], square(real, imag)).astype(BF)
        mask_grad = dot(rows, onto_y_ref[...]) * (1.0 / pixels)
        theta = theta_ref[i]
        gradient = mask_grad * (1.0 - jnp.tanh(theta) ** 2)
        new_first = beta_one * first_ref[i] + (1.0 - beta_one) * gradient
        new_second = beta_two * second_ref[i] + (1.0 - beta_two) * gradient * gradient
        new_theta = theta - learn_rate * (new_first / fix_ref[0]) / (
            jnp.sqrt(new_second / fix_ref[1]) + adam_eps
        )
        new_theta_ref[i] = new_theta
        new_first_ref[i] = new_first
        new_second_ref[i] = new_second
        if last:
            out_refs[0][i] = gradient
        else:
            out_refs[0][i], out_refs[1][i] = spectrum_part(
                core_ref[0], new_theta, across_y_ref[...], down_x_ref[...], band, pixels
            )


def field_kernel(
    core_ref,
    mine_ref,
    other_ref,
    kernels_ref,
    rows_ref,
    columns_ref,
    fields_ref,
    intensity_ref,
    half_ref,
):
    kernel_count = kernels_ref.shape[1]
    coarse = rows_ref.shape[0]
    first = core_ref[0] == 0

    def image(i):
        mine = mine_ref[i].astype(F32)
        other = other_ref[i].astype(F32)
        spectrum_real = jnp.where(first, mine, other)
        spectrum_imag = jnp.where(first, other, mine)
        for k in range(kernel_count):
            kernel_real = kernels_ref[0, k].astype(F32)
            kernel_imag = kernels_ref[1, k].astype(F32)
            real = (kernel_real * spectrum_real - kernel_imag * spectrum_imag).astype(BF)
            imag = (kernel_real * spectrum_imag + kernel_imag * spectrum_real).astype(BF)
            half_ref[k] = dot(rows_ref[...], square(real, imag)).astype(BF)
        total = None
        for k in range(kernel_count):
            field = dot(half_ref[k], columns_ref[...])
            fields_ref[i, k] = field.astype(BF)
            field_real, field_imag = field[:, :coarse], field[:, coarse:]
            power = field_real * field_real + field_imag * field_imag
            total = power if total is None else total + power
        intensity_ref[i] = total.astype(BF)

    for_each(fields_ref.shape[0], image)


def resist_kernel(
    own_ref, other_ref, sign_ref, up_x_ref, down_x_ref, up_y_ref, down_y_ref, out_ref, drive_ref
):
    pixels, coarse = up_x_ref.shape
    chunk = min(256, pixels)
    half_gain = 0.5 * resist_gain

    def image(i):
        intensity = (own_ref[i].astype(F32) + other_ref[i].astype(F32)).astype(BF)
        wide = dot(intensity, up_y_ref[...]).astype(BF)
        for start in range(0, pixels, chunk):
            fine = dot(up_x_ref[start : start + chunk, :], wide)
            bent = jnp.tanh(half_gain * fine - half_gain * resist_level)
            sign = sign_ref[start : start + chunk, :].astype(F32)
            drive = (bent + sign) * (1.0 - bent * bent)
            drive_ref[start : start + chunk, :] = drive.astype(BF)
        total = dot(down_x_ref[...], drive_ref[...])
        out_ref[i] = dot(total.astype(BF), down_y_ref[...]).astype(BF)

    for_each(own_ref.shape[0], image)


def adjoint_kernel(
    own_ref, other_ref, fields_ref, kernels_ref, columns_ref, rows_ref, out_ref, back_ref
):
    kernel_count = kernels_ref.shape[1]
    band = kernels_ref.shape[3]

    def image(i):
        drive = (own_ref[i].astype(F32) + other_ref[i].astype(F32)).astype(BF)
        drive_twice = jnp.concatenate([drive, drive], axis=1)
        for k in range(kernel_count):
            push = drive_twice * fields_ref[i, k]
            back_ref[k] = dot(push, columns_ref[...]).astype(BF)
        total_real = total_imag = None
        for k in range(kernel_count):
            parts = dot(rows_ref[...], back_ref[k])
            spectral_real = parts[:band, :band] + parts[band:, band:]
            spectral_imag = parts[:band, band:] - parts[band:, :band]
            kernel_real = kernels_ref[0, k].astype(F32)
            kernel_imag = kernels_ref[1, k].astype(F32)
            term_real = kernel_real * spectral_real + kernel_imag * spectral_imag
            term_imag = kernel_real * spectral_imag - kernel_imag * spectral_real
            total_real = term_real if total_real is None else total_real + term_real
            total_imag = term_imag if total_imag is None else total_imag + term_imag
        scale = 0.25 * resist_gain
        out_ref[0, i] = (scale * total_real).astype(BF)
        out_ref[1, i] = (scale * total_imag).astype(BF)

    for_each(own_ref.shape[0], image)


def swap(value, axis, mask):
    count = lax.axis_size(axis)
    return lax.ppermute(value, axis, [(i, i ^ mask) for i in range(count)])


def add(first, *others):
    total = first.astype(F32)
    for other in others:
        total = total + other.astype(F32)
    return total.astype(BF)


def sum_axis(value, axis, unit, count):
    if count <= 4:
        return add(value, *[swap(value, axis, unit * m) for m in range(1, count)])
    bit = 1
    while bit < count:
        value = add(value, swap(value, axis, unit * bit))
        bit *= 2
    return value


def body(mask_theta, first_moment, second_moment, target_bits, kernels, kernel_weights):
    tile_count, row_count, column_count = mask_theta.shape
    word_count = target_bits.shape[2]
    band = kernels.shape[-1]
    coarse = 2 * band
    tiles = lax.axis_size("tile")
    chips = lax.axis_size("kern") // 2
    pixels = tiles * row_count
    strip = chips * column_count
    step = pixels // coarse
    tile_at = lax.axis_index("tile")
    kern_at = lax.axis_index("kern")
    core = kern_at % 2
    core_scalar = core.astype(jnp.int32).reshape(1)

    def after(values, anchor):
        return lax.optimization_barrier((values, anchor))[0]

    fine_table = jnp.asarray(cos_sin(band, pixels, np.arange(pixels)), BF)
    coarse_rows = cos_sin(band, pixels, np.arange(coarse) * step)
    cos_c, sin_c = coarse_rows[:, :band], coarse_rows[:, band:]
    field_rows = jnp.asarray(coarse_rows, BF)
    field_columns = jnp.asarray(
        np.block([[cos_c.T, sin_c.T], [-sin_c.T, cos_c.T]]) / band, BF
    )
    back_columns = jnp.asarray(np.block([[cos_c, -sin_c], [sin_c, cos_c]]) * (2.0 / band), BF)
    back_rows = jnp.asarray(coarse_rows.T, BF)
    up_table = jnp.asarray(interpolation(coarse, pixels), BF)
    place = np.arange(strip) % column_count
    padded = -(-word_count // 8) * 8
    word_of = (np.arange(strip) // column_count) * padded + place // 30
    bit_of = place % 30
    picks = jnp.asarray(
        (
            (np.arange(chips * padded)[None, :, None] == word_of)
            & (np.arange(4)[:, None, None] == bit_of // 8)
        ).reshape(4 * chips * padded, strip),
        BF,
    )
    shift = jnp.asarray((bit_of % 8)[None, :], jnp.int32)

    row_start = tile_at * row_count
    column_start = kern_at * column_count
    along_x = lax.dynamic_slice_in_dim(fine_table, row_start, row_count, 0)
    down_x = along_x.T
    across_y = lax.dynamic_slice_in_dim(fine_table, column_start, column_count, 0)
    onto_y = jnp.concatenate([across_y.T[:band], -across_y.T[band:]])

    def spread(shape, dtype=BF):
        return jax.ShapeDtypeStruct(shape, dtype)

    mine, theirs = call(
        functools.partial(mask_kernel, band, pixels),
        [spread((tile_count, band, band))] * 2,
        (mask_theta, across_y, down_x),
        scalars=(core_scalar,),
        flops=tile_count * 10**8,
    )
    mine = add(mine, swap(theirs, "kern", 1))

    scaled = (after(kernels, mine) * jnp.sqrt(kernel_weights)[None, :, None, None]).astype(BF)
    mine = sum_axis(mine, "kern", 2, chips)
    words = jnp.swapaxes(after(target_bits, mine), 1, 2)
    own_kernels = jnp.concatenate(
        [scaled] + [swap(scaled, "kern", 2 * m) for m in range(1, chips)], axis=1
    )
    kernel_count = own_kernels.shape[1]
    mine = sum_axis(mine, "tile", 1, tiles)
    trade = swap(mine, "kern", 1)
    pieces = jnp.stack([words] + [swap(words, "tile", m) for m in range(1, tiles)])
    pieces = jnp.stack([pieces] + [swap(pieces, "kern", 2 * m) for m in range(1, chips)])
    pieces = jnp.pad(pieces, [(0, 0)] * 3 + [(0, padded - word_count), (0, 0)])

    up_table_t = up_table.T
    starts = [(kern_at ^ (2 * m)) * column_count for m in range(chips)]
    up_y = jnp.concatenate(
        [lax.dynamic_slice_in_dim(up_table_t, at, column_count, 1) for at in starts], axis=1
    )
    down_y = jnp.concatenate(
        [lax.dynamic_slice_in_dim(up_table, at, column_count, 0) for at in starts], axis=0
    )

    def unpack(i, anchor):
        return call(
            unpack_kernel,
            spread((pixels, strip)),
            (after(pieces, anchor), picks, shift),
            scalars=(tile_at.astype(jnp.int32).reshape(1), jnp.full((1,), i, jnp.int32)),
            flops=2 * 10**8,
        )

    signs = [None] * tile_count

    steps = range(first_step, first_step + ITERS)
    fixes = jnp.asarray([[1.0 - beta_one**s, 1.0 - beta_two**s] for s in steps], F32)

    def image(i, mine, trade, at):
        fields, intensity = call(
            field_kernel,
            [spread((1, kernel_count, coarse, 2 * coarse)), spread((1, coarse, coarse))],
            (mine[at : at + 1], trade[at : at + 1], own_kernels, field_rows, field_columns),
            scalars=(core_scalar,),
            scratch=[pltpu.VMEM((kernel_count, coarse, coarse), BF)],
            flops=10**9,
        )
        if signs[i] is None:
            signs[i] = unpack(i, intensity)
        drive = call(
            resist_kernel,
            spread((1, coarse, coarse)),
            (intensity, swap(intensity, "kern", 1), signs[i], up_table, up_table_t, up_y, down_y),
            scratch=[pltpu.VMEM((pixels, strip), BF)],
            flops=7 * 10**8,
        )
        adjoint = call(
            adjoint_kernel,
            spread((2, 1, band, band)),
            (drive, swap(drive, "kern", 1), fields, own_kernels, back_columns, back_rows),
            scratch=[pltpu.VMEM((kernel_count, coarse, coarse), BF)],
            flops=10**9,
        )
        return adjoint

    def update(iteration, group, state, mine, trade, last):
        block = spread((len(group), row_count, column_count), F32)
        half = spread((len(group), band, band))
        adjoints = [image(i, mine, trade, at) for at, i in enumerate(group)]
        if PAIRED and len(group) > 2:
            first = jnp.concatenate(adjoints[:-1], axis=1)
            adjoints = [first, swap(first, "kern", 1), adjoints[-1], swap(adjoints[-1], "kern", 1)]
        else:
            adjoints = sum([[a, swap(a, "kern", 1)] for a in adjoints], [])
        return call(
            functools.partial(update_kernel, band, pixels, last),
            [block] * 3 + ([block] if last else [half] * 2),
            (*adjoints, *state, along_x, onto_y, across_y, down_x),
            scalars=(core_scalar, fixes[iteration]),
            flops=6 * 10**8,
        )

    carries = []
    for group in GROUPS:
        part = slice(group[0], group[-1] + 1)
        state = [mask_theta[part], first_moment[part], second_moment[part]]
        carries.append((state, mine[part], trade[part]))
    for iteration in range(ITERS - 1):
        for g, group in enumerate(GROUPS):
            *state, mine, theirs = update(iteration, group, *carries[g], False)
            mine = add(mine, swap(theirs, "kern", 1))
            mine = sum_axis(mine, "kern", 2, chips)
            mine = sum_axis(mine, "tile", 1, tiles)
            carries[g] = state, mine, swap(mine, "kern", 1)
    results = [update(ITERS - 1, group, *carries[g], True) for g, group in enumerate(GROUPS)]
    return tuple(jnp.concatenate(outs) if len(outs) > 1 else outs[0] for outs in zip(*results))


def solution(mesh):
    block = P("grp", "tile", "kern")
    return jax.shard_map(
        body,
        mesh=mesh,
        in_specs=(block, block, block, block, P(None, "kern", None, None), P("kern")),
        out_specs=(block, block, block, block),
        check_vma=False,
    )
```

```python
import functools

import jax
import jax.numpy as jnp
import numpy as np
from jax import lax
from jax.experimental import pallas as pl
from jax.experimental.pallas import tpu as pltpu
from jax.sharding import PartitionSpec as P

ITERS = 4
GROUPS = (2, 1)
VMEM_LIMIT = 24 * 2**20

learn_rate = 0.1
beta_one = 0.9
beta_two = 0.999
adam_eps = 1e-08
first_step = 10
resist_gain = 3.0
resist_level = 1.0

BF = jnp.bfloat16
F32 = jnp.float32


def dot(left, right):
    return jnp.dot(left, right, preferred_element_type=F32)


def cos_sin(band, pixels, places):
    freq = np.arange(band, dtype=np.int64) - band // 2
    phase = (freq[None, :] * np.asarray(places, np.int64)[:, None]) % pixels
    angle = phase * (2.0 * np.pi / pixels)
    return np.concatenate([np.cos(angle), np.sin(angle)], axis=1)


def interpolation(coarse, pixels):
    step = pixels // coarse
    offset = (np.arange(pixels)[:, None] - step * np.arange(coarse)[None, :]) % pixels
    freq = np.arange(1, coarse // 2)
    kernel = 1.0 + 2.0 * np.cos(
        2.0 * np.pi * ((freq[None, :] * np.arange(pixels)[:, None]) % pixels) / pixels
    ).sum(axis=1)
    return kernel[offset] / coarse


def for_each(count, step):
    if count == 1:
        step(0)
    else:
        lax.fori_loop(0, count, lambda i, c: (step(i), c)[1], 0)


def call(body, out_shape, args, scratch=(), flops=0, scalars=(), limit=VMEM_LIMIT):
    vmem = pl.BlockSpec(memory_space=pltpu.VMEM)
    smem = pl.BlockSpec(memory_space=pltpu.SMEM)
    many = isinstance(out_shape, (list, tuple))
    nbytes = sum(int(np.prod(a.shape)) * a.dtype.itemsize for a in args)
    return pl.pallas_call(
        body,
        out_shape=out_shape,
        in_specs=[smem] * len(scalars) + [vmem] * len(args),
        out_specs=[vmem] * len(out_shape) if many else vmem,
        scratch_shapes=list(scratch),
        compiler_params=pltpu.CompilerParams(vmem_limit_bytes=limit),
        cost_estimate=pl.CostEstimate(flops=flops, bytes_accessed=nbytes, transcendentals=0),
    )(*scalars, *args)


def square(real, imag):
    return jnp.concatenate(
        [jnp.concatenate([real, imag], axis=1), jnp.concatenate([-imag, real], axis=1)], axis=0
    )


def unpack_kernel(at_ref, pieces_ref, picks_ref, shift_ref, sign_ref):
    chips, tiles, count, _, rows = pieces_ref.shape

    def image(i):
        for m in range(tiles):
            words = jnp.concatenate([pieces_ref[c, m, i] for c in range(chips)], axis=0)
            parts = [jnp.right_shift(words, 8 * q) & 255 for q in range(4)]
            octets = jnp.concatenate(parts, axis=0).astype(F32).astype(BF)
            value = lax.dot_general(
                octets, picks_ref[...], (((0,), (0,)), ((), ())), preferred_element_type=F32
            )
            bits = jnp.right_shift(value.astype(jnp.int32), shift_ref[...]) & 1
            start = pl.multiple_of((at_ref[0] ^ m) * rows, rows)
            sign_ref[i, pl.ds(start, rows), :] = (1 - 2 * bits).astype(F32).astype(BF)

    for_each(count, image)


def spectrum_part(core, theta, across_y, down_x, band, pixels):
    mask_bf = jnp.tanh(theta).astype(BF)
    across = dot(mask_bf, across_y).astype(BF)
    part = dot(down_x, across) * (1.0 / pixels)
    real = part[:band, :band] - part[band:, band:]
    imag = -(part[band:, :band] + part[:band, band:])
    first = core == 0
    return jnp.where(first, real, imag).astype(BF), jnp.where(first, imag, real).astype(BF)


def mask_kernel(band, pixels, core_ref, theta_ref, across_y_ref, down_x_ref, mine_ref, theirs_ref):
    for i in range(theta_ref.shape[0]):
        mine_ref[i], theirs_ref[i] = spectrum_part(
            core_ref[0], theta_ref[i], across_y_ref[...], down_x_ref[...], band, pixels
        )


def update_kernel(band, pixels, last, core_ref, fix_ref, *refs):
    split = len(refs) - 8 - (1 if last else 2)
    *adjoint_refs, theta_ref, first_ref, second_ref = refs[:split + 1]
    along_x_ref, onto_y_ref, across_y_ref, down_x_ref = refs[split + 1 : split + 5]
    new_theta_ref, new_first_ref, new_second_ref, *out_refs = refs[split + 5 :]
    pairs = []
    for own_ref, other_ref in zip(adjoint_refs[::2], adjoint_refs[1::2]):
        pairs += [(own_ref, other_ref, at) for at in range(own_ref.shape[1])]
    for i, (own_ref, other_ref, at) in enumerate(pairs):
        real = (own_ref[0, at].astype(F32) + other_ref[0, at].astype(F32)).astype(BF)
        imag = (own_ref[1, at].astype(F32) + other_ref[1, at].astype(F32)).astype(BF)
        rows = dot(along_x_ref[...], square(real, imag)).astype(BF)
        mask_grad = dot(rows, onto_y_ref[...]) * (1.0 / pixels)
        theta = theta_ref[i]
        gradient = mask_grad * (1.0 - jnp.tanh(theta) ** 2)
        new_first = beta_one * first_ref[i] + (1.0 - beta_one) * gradient
        new_second = beta_two * second_ref[i] + (1.0 - beta_two) * gradient * gradient
        new_theta = theta - learn_rate * (new_first / fix_ref[0]) / (
            jnp.sqrt(new_second / fix_ref[1]) + adam_eps
        )
        new_theta_ref[i] = new_theta
        new_first_ref[i] = new_first
        new_second_ref[i] = new_second
        if last:
            out_refs[0][i] = gradient
        else:
            out_refs[0][i], out_refs[1][i] = spectrum_part(
                core_ref[0], new_theta, across_y_ref[...], down_x_ref[...], band, pixels
            )


def field_kernel(
    core_ref,
    mine_ref,
    other_ref,
    kernels_ref,
    rows_ref,
    columns_ref,
    fields_ref,
    intensity_ref,
    half_ref,
):
    kernel_count = kernels_ref.shape[1]
    coarse = rows_ref.shape[0]
    first = core_ref[0] == 0

    def image(i):
        mine = mine_ref[i].astype(F32)
        other = other_ref[i].astype(F32)
        spectrum_real = jnp.where(first, mine, other)
        spectrum_imag = jnp.where(first, other, mine)
        for k in range(kernel_count):
            kernel_real = kernels_ref[0, k].astype(F32)
            kernel_imag = kernels_ref[1, k].astype(F32)
            real = (kernel_real * spectrum_real - kernel_imag * spectrum_imag).astype(BF)
            imag = (kernel_real * spectrum_imag + kernel_imag * spectrum_real).astype(BF)
            half_ref[k] = dot(rows_ref[...], square(real, imag)).astype(BF)
        total = None
        for k in range(kernel_count):
            field = dot(half_ref[k], columns_ref[...])
            fields_ref[i, k] = field.astype(BF)
            field_real, field_imag = field[:, :coarse], field[:, coarse:]
            power = field_real * field_real + field_imag * field_imag
            total = power if total is None else total + power
        intensity_ref[i] = total.astype(BF)

    for_each(fields_ref.shape[0], image)


def resist_kernel(
    own_ref, other_ref, sign_ref, up_x_ref, down_x_ref, up_y_ref, down_y_ref, out_ref, drive_ref
):
    pixels, coarse = up_x_ref.shape
    chunk = min(256, pixels)
    half_gain = 0.5 * resist_gain

    def image(i):
        intensity = (own_ref[i].astype(F32) + other_ref[i].astype(F32)).astype(BF)
        wide = dot(intensity, up_y_ref[...]).astype(BF)
        for start in range(0, pixels, chunk):
            fine = dot(up_x_ref[start : start + chunk, :], wide)
            bent = jnp.tanh(half_gain * fine - half_gain * resist_level)
            sign = sign_ref[i, start : start + chunk, :].astype(F32)
            drive = (bent + sign) * (1.0 - bent * bent)
            drive_ref[start : start + chunk, :] = drive.astype(BF)
        total = dot(down_x_ref[...], drive_ref[...])
        out_ref[i] = dot(total.astype(BF), down_y_ref[...]).astype(BF)

    for_each(own_ref.shape[0], image)


def adjoint_kernel(
    own_ref, other_ref, fields_ref, kernels_ref, columns_ref, rows_ref, out_ref, back_ref
):
    kernel_count = kernels_ref.shape[1]
    band = kernels_ref.shape[3]

    def image(i):
        drive = (own_ref[i].astype(F32) + other_ref[i].astype(F32)).astype(BF)
        drive_twice = jnp.concatenate([drive, drive], axis=1)
        for k in range(kernel_count):
            push = drive_twice * fields_ref[i, k]
            back_ref[k] = dot(push, columns_ref[...]).astype(BF)
        total_real = total_imag = None
        for k in range(kernel_count):
            parts = dot(rows_ref[...], back_ref[k])
            spectral_real = parts[:band, :band] + parts[band:, band:]
            spectral_imag = parts[:band, band:] - parts[band:, :band]
            kernel_real = kernels_ref[0, k].astype(F32)
            kernel_imag = kernels_ref[1, k].astype(F32)
            term_real = kernel_real * spectral_real + kernel_imag * spectral_imag
            term_imag = kernel_real * spectral_imag - kernel_imag * spectral_real
            total_real = term_real if total_real is None else total_real + term_real
            total_imag = term_imag if total_imag is None else total_imag + term_imag
        scale = 0.25 * resist_gain
        out_ref[0, i] = (scale * total_real).astype(BF)
        out_ref[1, i] = (scale * total_imag).astype(BF)

    for_each(own_ref.shape[0], image)


def swap(value, axis, mask):
    count = lax.axis_size(axis)
    return lax.ppermute(value, axis, [(i, i ^ mask) for i in range(count)])


def add(first, *others):
    total = first.astype(F32)
    for other in others:
        total = total + other.astype(F32)
    return total.astype(BF)


def sum_axis(value, axis, unit, count):
    if count <= 4:
        return add(value, *[swap(value, axis, unit * m) for m in range(1, count)])
    bit = 1
    while bit < count:
        value = add(value, swap(value, axis, unit * bit))
        bit *= 2
    return value


def body(mask_theta, first_moment, second_moment, target_bits, kernels, kernel_weights):
    tile_count, row_count, column_count = mask_theta.shape
    word_count = target_bits.shape[2]
    band = kernels.shape[-1]
    coarse = 2 * band
    tiles = lax.axis_size("tile")
    chips = lax.axis_size("kern") // 2
    pixels = tiles * row_count
    strip = chips * column_count
    step = pixels // coarse
    tile_at = lax.axis_index("tile")
    kern_at = lax.axis_index("kern")
    core = kern_at % 2
    core_scalar = core.astype(jnp.int32).reshape(1)

    def after(values, anchor):
        return lax.optimization_barrier((values, anchor))[0]

    fine_table = jnp.asarray(cos_sin(band, pixels, np.arange(pixels)), BF)
    coarse_rows = cos_sin(band, pixels, np.arange(coarse) * step)
    cos_c, sin_c = coarse_rows[:, :band], coarse_rows[:, band:]
    field_rows = jnp.asarray(coarse_rows, BF)
    field_columns = jnp.asarray(
        np.block([[cos_c.T, sin_c.T], [-sin_c.T, cos_c.T]]) / band, BF
    )
    back_columns = jnp.asarray(np.block([[cos_c, -sin_c], [sin_c, cos_c]]) * (2.0 / band), BF)
    back_rows = jnp.asarray(coarse_rows.T, BF)
    up_table = jnp.asarray(interpolation(coarse, pixels), BF)
    place = np.arange(strip) % column_count
    padded = -(-word_count // 8) * 8
    word_of = (np.arange(strip) // column_count) * padded + place // 30
    bit_of = place % 30
    picks = jnp.asarray(
        (
            (np.arange(chips * padded)[None, :, None] == word_of)
            & (np.arange(4)[:, None, None] == bit_of // 8)
        ).reshape(4 * chips * padded, strip),
        BF,
    )
    shift = jnp.asarray((bit_of % 8)[None, :], jnp.int32)

    row_start = tile_at * row_count
    column_start = kern_at * column_count
    along_x = lax.dynamic_slice_in_dim(fine_table, row_start, row_count, 0)
    down_x = along_x.T
    across_y = lax.dynamic_slice_in_dim(fine_table, column_start, column_count, 0)
    onto_y = jnp.concatenate([across_y.T[:band], -across_y.T[band:]])

    def spread(shape, dtype=BF):
        return jax.ShapeDtypeStruct(shape, dtype)

    mine, theirs = call(
        functools.partial(mask_kernel, band, pixels),
        [spread((tile_count, band, band))] * 2,
        (mask_theta, across_y, down_x),
        scalars=(core_scalar,),
        flops=tile_count * 10**8,
    )
    mine = add(mine, swap(theirs, "kern", 1))

    scaled = (after(kernels, mine) * jnp.sqrt(kernel_weights)[None, :, None, None]).astype(BF)
    mine = sum_axis(mine, "kern", 2, chips)
    words = jnp.swapaxes(after(target_bits, mine), 1, 2)
    own_kernels = jnp.concatenate(
        [scaled] + [swap(scaled, "kern", 2 * m) for m in range(1, chips)], axis=1
    )
    kernel_count = own_kernels.shape[1]
    mine = sum_axis(mine, "tile", 1, tiles)
    trade = swap(mine, "kern", 1)
    pieces = jnp.stack([words] + [swap(words, "tile", m) for m in range(1, tiles)])
    pieces = jnp.stack([pieces] + [swap(pieces, "kern", 2 * m) for m in range(1, chips)])
    pieces = jnp.pad(pieces, [(0, 0)] * 3 + [(0, padded - word_count), (0, 0)])

    up_table_t = up_table.T
    starts = [(kern_at ^ (2 * m)) * column_count for m in range(chips)]
    up_y = jnp.concatenate(
        [lax.dynamic_slice_in_dim(up_table_t, at, column_count, 1) for at in starts], axis=1
    )
    down_y = jnp.concatenate(
        [lax.dynamic_slice_in_dim(up_table, at, column_count, 0) for at in starts], axis=0
    )

    groups = []
    for size in GROUPS:
        start = groups[-1].stop if groups else 0
        groups.append(slice(start, min(start + size, tile_count)))

    def unpack(group, anchor):
        return call(
            unpack_kernel,
            spread((group.stop - group.start, pixels, strip)),
            (after(pieces[:, :, group], anchor), picks, shift),
            scalars=(tile_at.astype(jnp.int32).reshape(1),),
            flops=2 * 10**8,
        )

    signs = [None] * len(groups)

    steps = range(first_step, first_step + ITERS)
    fixes = jnp.asarray([[1.0 - beta_one**s, 1.0 - beta_two**s] for s in steps], F32)

    def traded(values):
        return [(value, after(swap(value, "kern", 1), values[-1])) for value in values]

    def adjoints(mine, trade):
        counts = [group.stop - group.start for group in groups]
        fields, values = [], []
        for group, count in zip(groups, counts):
            field, intensity = call(
                field_kernel,
                [
                    spread((count, kernel_count, coarse, 2 * coarse)),
                    spread((count, coarse, coarse)),
                ],
                (mine[group], trade[group], own_kernels, field_rows, field_columns),
                scalars=(core_scalar,),
                scratch=[pltpu.VMEM((kernel_count, coarse, coarse), BF)],
                flops=count * 10**9,
            )
            fields.append(field)
            values.append(intensity)
        for g, group in enumerate(groups):
            if signs[g] is None:
                signs[g] = unpack(group, values[-1])
        values = [
            call(
                resist_kernel,
                spread((count, coarse, coarse)),
                (*pair, sign, up_table, up_table_t, up_y, down_y),
                scratch=[pltpu.VMEM((pixels, strip), BF)],
                flops=count * 7 * 10**8,
            )
            for count, pair, sign in zip(counts, traded(values), signs)
        ]
        values = [
            call(
                adjoint_kernel,
                spread((2, count, band, band)),
                (*pair, field, own_kernels, back_columns, back_rows),
                scratch=[pltpu.VMEM((kernel_count, coarse, coarse), BF)],
                flops=count * 10**9,
            )
            for count, pair, field in zip(counts, traded(values), fields)
        ]
        return sum([[value, swap(value, "kern", 1)] for value in values], [])

    block = spread(mask_theta.shape, F32)
    half = spread((tile_count, band, band))
    state = [mask_theta, first_moment, second_moment]
    for iteration in range(ITERS):
        last = iteration == ITERS - 1
        pairs = adjoints(mine, trade)
        outs = call(
            functools.partial(update_kernel, band, pixels, last),
            [block] * 3 + ([block] if last else [half] * 2),
            (*pairs, *state, along_x, onto_y, across_y, down_x),
            scalars=(core_scalar, fixes[iteration]),
            flops=6 * 10**8,
        )
        if last:
            return tuple(outs)
        state, (mine, theirs) = outs[:3], outs[3:]
        mine = add(mine, swap(theirs, "kern", 1))
        mine = sum_axis(mine, "kern", 2, chips)
        mine = sum_axis(mine, "tile", 1, tiles)
        trade = swap(mine, "kern", 1)


def solution(mesh):
    block = P("grp", "tile", "kern")
    return jax.shard_map(
        body,
        mesh=mesh,
        in_specs=(block, block, block, block, P(None, "kern", None, None), P("kern")),
        out_specs=(block, block, block, block),
        check_vma=False,
    )
```

```python
import functools

import jax
import jax.numpy as jnp
import numpy as np
from jax import lax
from jax.experimental import pallas as pl
from jax.experimental.pallas import tpu as pltpu
from jax.sharding import PartitionSpec as P

ITERS = 4
GROUPS = (2, 1)
VMEM_LIMIT = 24 * 2**20

learn_rate = 0.1
beta_one = 0.9
beta_two = 0.999
adam_eps = 1e-08
first_step = 10
resist_gain = 3.0
resist_level = 1.0

BF = jnp.bfloat16
F32 = jnp.float32


def dot(left, right):
    return jnp.dot(left, right, preferred_element_type=F32)


def cos_sin(band, pixels, places):
    freq = np.arange(band, dtype=np.int64) - band // 2
    phase = (freq[None, :] * np.asarray(places, np.int64)[:, None]) % pixels
    angle = phase * (2.0 * np.pi / pixels)
    return np.concatenate([np.cos(angle), np.sin(angle)], axis=1)


def interpolation(coarse, pixels):
    step = pixels // coarse
    offset = (np.arange(pixels)[:, None] - step * np.arange(coarse)[None, :]) % pixels
    freq = np.arange(1, coarse // 2)
    kernel = 1.0 + 2.0 * np.cos(
        2.0 * np.pi * ((freq[None, :] * np.arange(pixels)[:, None]) % pixels) / pixels
    ).sum(axis=1)
    return kernel[offset] / coarse


def for_each(count, step):
    if count == 1:
        step(0)
    else:
        lax.fori_loop(0, count, lambda i, c: (step(i), c)[1], 0)


def call(body, out_shape, args, scratch=(), flops=0, scalars=(), limit=VMEM_LIMIT):
    vmem = pl.BlockSpec(memory_space=pltpu.VMEM)
    smem = pl.BlockSpec(memory_space=pltpu.SMEM)
    many = isinstance(out_shape, (list, tuple))
    nbytes = sum(int(np.prod(a.shape)) * a.dtype.itemsize for a in args)
    return pl.pallas_call(
        body,
        out_shape=out_shape,
        in_specs=[smem] * len(scalars) + [vmem] * len(args),
        out_specs=[vmem] * len(out_shape) if many else vmem,
        scratch_shapes=list(scratch),
        compiler_params=pltpu.CompilerParams(vmem_limit_bytes=limit),
        cost_estimate=pl.CostEstimate(flops=flops, bytes_accessed=nbytes, transcendentals=0),
    )(*scalars, *args)


def square(real, imag):
    return jnp.concatenate(
        [jnp.concatenate([real, imag], axis=1), jnp.concatenate([-imag, real], axis=1)], axis=0
    )


def unpack_kernel(at_ref, pieces_ref, picks_ref, shift_ref, *sign_refs):
    chips, tiles, count, _, rows = pieces_ref.shape
    starts = [sum(ref.shape[0] for ref in sign_refs[:g]) for g in range(len(sign_refs))]

    def piece(m):
        start = pl.multiple_of((at_ref[0] ^ m) * rows, rows)
        for first, sign_ref in zip(starts, sign_refs):
            for i in range(sign_ref.shape[0]):
                words = jnp.concatenate(
                    [pieces_ref[c, m, first + i] for c in range(chips)], axis=0
                )
                parts = [jnp.right_shift(words, 8 * q) & 255 for q in range(4)]
                octets = jnp.concatenate(parts, axis=0).astype(F32).astype(BF)
                value = lax.dot_general(
                    octets, picks_ref[...], (((0,), (0,)), ((), ())), preferred_element_type=F32
                )
                bits = jnp.right_shift(value.astype(jnp.int32), shift_ref[...]) & 1
                sign_ref[i, pl.ds(start, rows), :] = (1 - 2 * bits).astype(F32).astype(BF)

    for_each(tiles, piece)


def spectrum_part(core, theta, across_y, down_x, band, pixels):
    mask_bf = jnp.tanh(theta).astype(BF)
    across = dot(mask_bf, across_y).astype(BF)
    part = dot(down_x, across) * (1.0 / pixels)
    real = part[:band, :band] - part[band:, band:]
    imag = -(part[band:, :band] + part[:band, band:])
    first = core == 0
    return jnp.where(first, real, imag).astype(BF), jnp.where(first, imag, real).astype(BF)


def mask_kernel(band, pixels, core_ref, theta_ref, across_y_ref, down_x_ref, mine_ref, theirs_ref):
    def image(i):
        mine_ref[i], theirs_ref[i] = spectrum_part(
            core_ref[0], theta_ref[i], across_y_ref[...], down_x_ref[...], band, pixels
        )

    for_each(theta_ref.shape[0], image)


def update_kernel(band, pixels, last, core_ref, fix_ref, *refs):
    split = len(refs) - 9 - (1 if last else 2)
    *adjoint_refs, theta_ref, first_ref, second_ref = refs[:split + 1]
    along_x_ref, onto_y_ref, across_y_ref, down_x_ref = refs[split + 1 : split + 5]
    new_theta_ref, new_first_ref, new_second_ref, *out_refs, adjoint_ref = refs[split + 5 :]
    groups = list(zip(adjoint_refs[::2], adjoint_refs[1::2]))
    starts = [sum(own_ref.shape[1] for own_ref, _ in groups[:g]) for g in range(len(groups))]
    count = theta_ref.shape[0]
    for g, (own_ref, other_ref) in enumerate(groups):
        group = slice(starts[g], starts[g] + own_ref.shape[1])
        adjoint_ref[:, group] = (own_ref[...].astype(F32) + other_ref[...].astype(F32)).astype(BF)

    def image(i):
        real, imag = adjoint_ref[0, i], adjoint_ref[1, i]
        rows = dot(along_x_ref[...], square(real, imag)).astype(BF)
        mask_grad = dot(rows, onto_y_ref[...]) * (1.0 / pixels)
        theta = theta_ref[i]
        gradient = mask_grad * (1.0 - jnp.tanh(theta) ** 2)
        new_first = beta_one * first_ref[i] + (1.0 - beta_one) * gradient
        new_second = beta_two * second_ref[i] + (1.0 - beta_two) * gradient * gradient
        new_theta = theta - learn_rate * (new_first / fix_ref[0]) / (
            jnp.sqrt(new_second / fix_ref[1]) + adam_eps
        )
        new_theta_ref[i] = new_theta
        new_first_ref[i] = new_first
        new_second_ref[i] = new_second
        if last:
            out_refs[0][i] = gradient
        else:
            out_refs[0][i], out_refs[1][i] = spectrum_part(
                core_ref[0], new_theta, across_y_ref[...], down_x_ref[...], band, pixels
            )

    for_each(count, image)


def field_kernel(
    core_ref,
    mine_ref,
    other_ref,
    kernels_ref,
    rows_ref,
    columns_ref,
    fields_ref,
    intensity_ref,
    half_ref,
):
    kernel_count = kernels_ref.shape[1]
    coarse = rows_ref.shape[0]
    first = core_ref[0] == 0

    def image(i):
        mine = mine_ref[i].astype(F32)
        other = other_ref[i].astype(F32)
        spectrum_real = jnp.where(first, mine, other)
        spectrum_imag = jnp.where(first, other, mine)
        for k in range(kernel_count):
            kernel_real = kernels_ref[0, k].astype(F32)
            kernel_imag = kernels_ref[1, k].astype(F32)
            real = (kernel_real * spectrum_real - kernel_imag * spectrum_imag).astype(BF)
            imag = (kernel_real * spectrum_imag + kernel_imag * spectrum_real).astype(BF)
            half_ref[k] = dot(rows_ref[...], square(real, imag)).astype(BF)
        total = None
        for k in range(kernel_count):
            field = dot(half_ref[k], columns_ref[...])
            fields_ref[i, k] = field.astype(BF)
            field_real, field_imag = field[:, :coarse], field[:, coarse:]
            power = field_real * field_real + field_imag * field_imag
            total = power if total is None else total + power
        intensity_ref[i] = total.astype(BF)

    for_each(fields_ref.shape[0], image)


def resist_kernel(
    own_ref, other_ref, sign_ref, up_x_ref, down_x_ref, up_y_ref, down_y_ref, out_ref, drive_ref
):
    pixels, coarse = up_x_ref.shape
    chunk = min(256, pixels)
    half_gain = 0.5 * resist_gain

    def image(i):
        intensity = (own_ref[i].astype(F32) + other_ref[i].astype(F32)).astype(BF)
        wide = dot(intensity, up_y_ref[...]).astype(BF)
        for start in range(0, pixels, chunk):
            fine = dot(up_x_ref[start : start + chunk, :], wide)
            bent = jnp.tanh(half_gain * fine - half_gain * resist_level)
            sign = sign_ref[i, start : start + chunk, :].astype(F32)
            drive = (bent + sign) * (1.0 - bent * bent)
            drive_ref[start : start + chunk, :] = drive.astype(BF)
        total = dot(down_x_ref[...], drive_ref[...])
        out_ref[i] = dot(total.astype(BF), down_y_ref[...]).astype(BF)

    for_each(own_ref.shape[0], image)


def adjoint_kernel(
    own_ref, other_ref, fields_ref, kernels_ref, columns_ref, rows_ref, out_ref, back_ref
):
    kernel_count = kernels_ref.shape[1]
    band = kernels_ref.shape[3]

    def image(i):
        drive = (own_ref[i].astype(F32) + other_ref[i].astype(F32)).astype(BF)
        drive_twice = jnp.concatenate([drive, drive], axis=1)
        for k in range(kernel_count):
            push = drive_twice * fields_ref[i, k]
            back_ref[k] = dot(push, columns_ref[...]).astype(BF)
        total_real = total_imag = None
        for k in range(kernel_count):
            parts = dot(rows_ref[...], back_ref[k])
            spectral_real = parts[:band, :band] + parts[band:, band:]
            spectral_imag = parts[:band, band:] - parts[band:, :band]
            kernel_real = kernels_ref[0, k].astype(F32)
            kernel_imag = kernels_ref[1, k].astype(F32)
            term_real = kernel_real * spectral_real + kernel_imag * spectral_imag
            term_imag = kernel_real * spectral_imag - kernel_imag * spectral_real
            total_real = term_real if total_real is None else total_real + term_real
            total_imag = term_imag if total_imag is None else total_imag + term_imag
        scale = 0.25 * resist_gain
        out_ref[0, i] = (scale * total_real).astype(BF)
        out_ref[1, i] = (scale * total_imag).astype(BF)

    for_each(own_ref.shape[0], image)


def swap(value, axis, mask):
    count = lax.axis_size(axis)
    return lax.ppermute(value, axis, [(i, i ^ mask) for i in range(count)])


def add(first, *others):
    total = first.astype(F32)
    for other in others:
        total = total + other.astype(F32)
    return total.astype(BF)


def sum_axis(value, axis, unit, count):
    if count <= 4:
        return add(value, *[swap(value, axis, unit * m) for m in range(1, count)])
    bit = 1
    while bit < count:
        value = add(value, swap(value, axis, unit * bit))
        bit *= 2
    return value


def body(mask_theta, first_moment, second_moment, target_bits, kernels, kernel_weights):
    tile_count, row_count, column_count = mask_theta.shape
    word_count = target_bits.shape[2]
    band = kernels.shape[-1]
    coarse = 2 * band
    tiles = lax.axis_size("tile")
    chips = lax.axis_size("kern") // 2
    pixels = tiles * row_count
    strip = chips * column_count
    step = pixels // coarse
    tile_at = lax.axis_index("tile")
    kern_at = lax.axis_index("kern")
    core = kern_at % 2
    core_scalar = core.astype(jnp.int32).reshape(1)

    def after(values, anchor):
        return lax.optimization_barrier((values, anchor))[0]

    fine_table = jnp.asarray(cos_sin(band, pixels, np.arange(pixels)), BF)
    coarse_rows = cos_sin(band, pixels, np.arange(coarse) * step)
    cos_c, sin_c = coarse_rows[:, :band], coarse_rows[:, band:]
    field_rows = jnp.asarray(coarse_rows, BF)
    field_columns = jnp.asarray(
        np.block([[cos_c.T, sin_c.T], [-sin_c.T, cos_c.T]]) / band, BF
    )
    back_columns = jnp.asarray(np.block([[cos_c, -sin_c], [sin_c, cos_c]]) * (2.0 / band), BF)
    back_rows = jnp.asarray(coarse_rows.T, BF)
    up_table = jnp.asarray(interpolation(coarse, pixels), BF)
    place = np.arange(strip) % column_count
    padded = -(-word_count // 8) * 8
    word_of = (np.arange(strip) // column_count) * padded + place // 30
    bit_of = place % 30
    picks = jnp.asarray(
        (
            (np.arange(chips * padded)[None, :, None] == word_of)
            & (np.arange(4)[:, None, None] == bit_of // 8)
        ).reshape(4 * chips * padded, strip),
        BF,
    )
    shift = jnp.asarray((bit_of % 8)[None, :], jnp.int32)

    row_start = tile_at * row_count
    column_start = kern_at * column_count
    along_x = lax.dynamic_slice_in_dim(fine_table, row_start, row_count, 0)
    down_x = along_x.T
    across_y = lax.dynamic_slice_in_dim(fine_table, column_start, column_count, 0)
    onto_y = jnp.concatenate([across_y.T[:band], -across_y.T[band:]])

    def spread(shape, dtype=BF):
        return jax.ShapeDtypeStruct(shape, dtype)

    mine, theirs = call(
        functools.partial(mask_kernel, band, pixels),
        [spread((tile_count, band, band))] * 2,
        (mask_theta, across_y, down_x),
        scalars=(core_scalar,),
        flops=tile_count * 10**8,
    )
    mine = add(mine, swap(theirs, "kern", 1))

    scaled = (after(kernels, mine) * jnp.sqrt(kernel_weights)[None, :, None, None]).astype(BF)
    mine = sum_axis(mine, "kern", 2, chips)
    words = jnp.swapaxes(after(target_bits, mine), 1, 2)
    own_kernels = jnp.concatenate(
        [scaled] + [swap(scaled, "kern", 2 * m) for m in range(1, chips)], axis=1
    )
    kernel_count = own_kernels.shape[1]
    mine = sum_axis(mine, "tile", 1, tiles)
    trade = swap(mine, "kern", 1)
    pieces = jnp.stack([words] + [swap(words, "tile", m) for m in range(1, tiles)])
    pieces = jnp.stack([pieces] + [swap(pieces, "kern", 2 * m) for m in range(1, chips)])
    pieces = jnp.pad(pieces, [(0, 0)] * 3 + [(0, padded - word_count), (0, 0)])

    up_table_t = up_table.T
    starts = [(kern_at ^ (2 * m)) * column_count for m in range(chips)]
    up_y = jnp.concatenate(
        [lax.dynamic_slice_in_dim(up_table_t, at, column_count, 1) for at in starts], axis=1
    )
    down_y = jnp.concatenate(
        [lax.dynamic_slice_in_dim(up_table, at, column_count, 0) for at in starts], axis=0
    )

    groups = []
    for size in GROUPS:
        start = groups[-1].stop if groups else 0
        groups.append(slice(start, min(start + size, tile_count)))

    def unpack(anchor):
        everything = call(
            unpack_kernel,
            [spread((group.stop - group.start, pixels, strip)) for group in groups],
            (after(pieces, anchor), picks, shift),
            scalars=(tile_at.astype(jnp.int32).reshape(1),),
            flops=6 * 10**8,
        )
        return everything

    signs = []

    steps = range(first_step, first_step + ITERS)
    fixes = jnp.asarray([[1.0 - beta_one**s, 1.0 - beta_two**s] for s in steps], F32)

    def traded(values):
        return [(value, after(swap(value, "kern", 1), values[-1])) for value in values]

    def adjoints(mine, trade):
        counts = [group.stop - group.start for group in groups]
        fields, values = [], []
        for group, count in zip(groups, counts):
            field, intensity = call(
                field_kernel,
                [
                    spread((count, kernel_count, coarse, 2 * coarse)),
                    spread((count, coarse, coarse)),
                ],
                (mine[group], trade[group], own_kernels, field_rows, field_columns),
                scalars=(core_scalar,),
                scratch=[pltpu.VMEM((kernel_count, coarse, coarse), BF)],
                flops=count * 10**9,
            )
            fields.append(field)
            values.append(intensity)
        if not signs:
            signs.extend(unpack(values[-1]))
        values = [
            call(
                resist_kernel,
                spread((count, coarse, coarse)),
                (*pair, sign, up_table, up_table_t, up_y, down_y),
                scratch=[pltpu.VMEM((pixels, strip), BF)],
                flops=count * 7 * 10**8,
            )
            for count, pair, sign in zip(counts, traded(values), signs)
        ]
        values = [
            call(
                adjoint_kernel,
                spread((2, count, band, band)),
                (*pair, field, own_kernels, back_columns, back_rows),
                scratch=[pltpu.VMEM((kernel_count, coarse, coarse), BF)],
                flops=count * 10**9,
            )
            for count, pair, field in zip(counts, traded(values), fields)
        ]
        return sum([[value, swap(value, "kern", 1)] for value in values], [])

    block = spread(mask_theta.shape, F32)
    half = spread((tile_count, band, band))
    state = [mask_theta, first_moment, second_moment]
    for iteration in range(ITERS):
        last = iteration == ITERS - 1
        pairs = adjoints(mine, trade)
        outs = call(
            functools.partial(update_kernel, band, pixels, last),
            [block] * 3 + ([block] if last else [half] * 2),
            (*pairs, *state, along_x, onto_y, across_y, down_x),
            scalars=(core_scalar, fixes[iteration]),
            scratch=[pltpu.VMEM((2, tile_count, band, band), BF)],
            flops=6 * 10**8,
        )
        if last:
            return tuple(outs)
        state, (mine, theirs) = outs[:3], outs[3:]
        mine = add(mine, swap(theirs, "kern", 1))
        mine = sum_axis(mine, "kern", 2, chips)
        mine = sum_axis(mine, "tile", 1, tiles)
        trade = swap(mine, "kern", 1)


def solution(mesh):
    block = P("grp", "tile", "kern")
    return jax.shard_map(
        body,
        mesh=mesh,
        in_specs=(block, block, block, block, P(None, "kern", None, None), P("kern")),
        out_specs=(block, block, block, block),
        check_vma=False,
    )
```

```python
import functools

import jax
import jax.numpy as jnp
import numpy as np
from jax import lax
from jax.experimental import pallas as pl
from jax.experimental.pallas import tpu as pltpu
from jax.sharding import PartitionSpec as P

ITERS = 4
GROUPS = (1, 2)
VMEM_LIMIT = 24 * 2**20

learn_rate = 0.1
beta_one = 0.9
beta_two = 0.999
adam_eps = 1e-08
first_step = 10
resist_gain = 3.0
resist_level = 1.0

BF = jnp.bfloat16
F32 = jnp.float32


def dot(left, right):
    return jnp.dot(left, right, preferred_element_type=F32)


def cos_sin(band, pixels, places):
    freq = np.arange(band, dtype=np.int64) - band // 2
    phase = (freq[None, :] * np.asarray(places, np.int64)[:, None]) % pixels
    angle = phase * (2.0 * np.pi / pixels)
    return np.concatenate([np.cos(angle), np.sin(angle)], axis=1)


def interpolation(coarse, pixels):
    step = pixels // coarse
    offset = (np.arange(pixels)[:, None] - step * np.arange(coarse)[None, :]) % pixels
    freq = np.arange(1, coarse // 2)
    kernel = 1.0 + 2.0 * np.cos(
        2.0 * np.pi * ((freq[None, :] * np.arange(pixels)[:, None]) % pixels) / pixels
    ).sum(axis=1)
    return kernel[offset] / coarse


def for_each(count, step):
    if count == 1:
        step(0)
    else:
        lax.fori_loop(0, count, lambda i, c: (step(i), c)[1], 0)


def call(body, out_shape, args, scratch=(), flops=0, scalars=(), limit=VMEM_LIMIT):
    vmem = pl.BlockSpec(memory_space=pltpu.VMEM)
    smem = pl.BlockSpec(memory_space=pltpu.SMEM)
    many = isinstance(out_shape, (list, tuple))
    nbytes = sum(int(np.prod(a.shape)) * a.dtype.itemsize for a in args)
    return pl.pallas_call(
        body,
        out_shape=out_shape,
        in_specs=[smem] * len(scalars) + [vmem] * len(args),
        out_specs=[vmem] * len(out_shape) if many else vmem,
        scratch_shapes=list(scratch),
        compiler_params=pltpu.CompilerParams(vmem_limit_bytes=limit),
        cost_estimate=pl.CostEstimate(flops=flops, bytes_accessed=nbytes, transcendentals=0),
    )(*scalars, *args)


def square(real, imag):
    return jnp.concatenate(
        [jnp.concatenate([real, imag], axis=1), jnp.concatenate([-imag, real], axis=1)], axis=0
    )


def unpack_kernel(at_ref, pieces_ref, picks_ref, shift_ref, *sign_refs):
    chips, tiles, count, _, rows = pieces_ref.shape
    starts = [sum(ref.shape[0] for ref in sign_refs[:g]) for g in range(len(sign_refs))]

    def piece(m):
        start = pl.multiple_of((at_ref[0] ^ m) * rows, rows)
        for first, sign_ref in zip(starts, sign_refs):
            for i in range(sign_ref.shape[0]):
                words = jnp.concatenate(
                    [pieces_ref[c, m, first + i] for c in range(chips)], axis=0
                )
                parts = [jnp.right_shift(words, 8 * q) & 255 for q in range(4)]
                octets = jnp.concatenate(parts, axis=0).astype(F32).astype(BF)
                value = lax.dot_general(
                    octets, picks_ref[...], (((0,), (0,)), ((), ())), preferred_element_type=F32
                )
                bits = jnp.right_shift(value.astype(jnp.int32), shift_ref[...]) & 1
                sign_ref[i, pl.ds(start, rows), :] = (1 - 2 * bits).astype(F32).astype(BF)

    for_each(tiles, piece)


def spectrum_part(core, theta, across_y, down_x, band, pixels):
    mask_bf = jnp.tanh(theta).astype(BF)
    across = dot(mask_bf, across_y).astype(BF)
    part = dot(down_x, across) * (1.0 / pixels)
    real = part[:band, :band] - part[band:, band:]
    imag = -(part[band:, :band] + part[:band, band:])
    first = core == 0
    return jnp.where(first, real, imag).astype(BF), jnp.where(first, imag, real).astype(BF)


def mask_kernel(band, pixels, core_ref, theta_ref, across_y_ref, down_x_ref, mine_ref, theirs_ref):
    def image(i):
        mine_ref[i], theirs_ref[i] = spectrum_part(
            core_ref[0], theta_ref[i], across_y_ref[...], down_x_ref[...], band, pixels
        )

    for_each(theta_ref.shape[0], image)


def update_kernel(band, pixels, last, core_ref, fix_ref, *refs):
    split = len(refs) - 9 - (1 if last else 2)
    *adjoint_refs, theta_ref, first_ref, second_ref = refs[:split + 1]
    along_x_ref, onto_y_ref, across_y_ref, down_x_ref = refs[split + 1 : split + 5]
    new_theta_ref, new_first_ref, new_second_ref, *out_refs, adjoint_ref = refs[split + 5 :]
    groups = list(zip(adjoint_refs[::2], adjoint_refs[1::2]))
    starts = [sum(own_ref.shape[1] for own_ref, _ in groups[:g]) for g in range(len(groups))]
    count = theta_ref.shape[0]
    for g, (own_ref, other_ref) in enumerate(groups):
        group = slice(starts[g], starts[g] + own_ref.shape[1])
        adjoint_ref[:, group] = (own_ref[...].astype(F32) + other_ref[...].astype(F32)).astype(BF)

    def image(i):
        real, imag = adjoint_ref[0, i], adjoint_ref[1, i]
        rows = dot(along_x_ref[...], square(real, imag)).astype(BF)
        mask_grad = dot(rows, onto_y_ref[...]) * (1.0 / pixels)
        theta = theta_ref[i]
        gradient = mask_grad * (1.0 - jnp.tanh(theta) ** 2)
        new_first = beta_one * first_ref[i] + (1.0 - beta_one) * gradient
        new_second = beta_two * second_ref[i] + (1.0 - beta_two) * gradient * gradient
        new_theta = theta - learn_rate * (new_first / fix_ref[0]) / (
            jnp.sqrt(new_second / fix_ref[1]) + adam_eps
        )
        new_theta_ref[i] = new_theta
        new_first_ref[i] = new_first
        new_second_ref[i] = new_second
        if last:
            out_refs[0][i] = gradient
        else:
            out_refs[0][i], out_refs[1][i] = spectrum_part(
                core_ref[0], new_theta, across_y_ref[...], down_x_ref[...], band, pixels
            )

    for_each(count, image)


def field_kernel(
    core_ref,
    mine_ref,
    other_ref,
    kernels_ref,
    rows_ref,
    columns_ref,
    fields_ref,
    intensity_ref,
    half_ref,
):
    kernel_count = kernels_ref.shape[1]
    coarse = rows_ref.shape[0]
    first = core_ref[0] == 0

    def image(i):
        mine = mine_ref[i].astype(F32)
        other = other_ref[i].astype(F32)
        spectrum_real = jnp.where(first, mine, other)
        spectrum_imag = jnp.where(first, other, mine)
        for k in range(kernel_count):
            kernel_real = kernels_ref[0, k].astype(F32)
            kernel_imag = kernels_ref[1, k].astype(F32)
            real = (kernel_real * spectrum_real - kernel_imag * spectrum_imag).astype(BF)
            imag = (kernel_real * spectrum_imag + kernel_imag * spectrum_real).astype(BF)
            half_ref[k] = dot(rows_ref[...], square(real, imag)).astype(BF)
        total = None
        for k in range(kernel_count):
            field = dot(half_ref[k], columns_ref[...])
            fields_ref[i, k] = field.astype(BF)
            field_real, field_imag = field[:, :coarse], field[:, coarse:]
            power = field_real * field_real + field_imag * field_imag
            total = power if total is None else total + power
        intensity_ref[i] = total.astype(BF)

    for_each(fields_ref.shape[0], image)


def resist_kernel(
    own_ref, other_ref, sign_ref, up_x_ref, down_x_ref, up_y_ref, down_y_ref, out_ref, drive_ref
):
    pixels, coarse = up_x_ref.shape
    chunk = min(256, pixels)
    half_gain = 0.5 * resist_gain

    def image(i):
        intensity = (own_ref[i].astype(F32) + other_ref[i].astype(F32)).astype(BF)
        wide = dot(intensity, up_y_ref[...]).astype(BF)
        for start in range(0, pixels, chunk):
            fine = dot(up_x_ref[start : start + chunk, :], wide)
            bent = jnp.tanh(half_gain * fine - half_gain * resist_level)
            sign = sign_ref[i, start : start + chunk, :].astype(F32)
            drive = (bent + sign) * (1.0 - bent * bent)
            drive_ref[start : start + chunk, :] = drive.astype(BF)
        total = dot(down_x_ref[...], drive_ref[...])
        out_ref[i] = dot(total.astype(BF), down_y_ref[...]).astype(BF)

    for_each(own_ref.shape[0], image)


def adjoint_kernel(
    own_ref, other_ref, fields_ref, kernels_ref, columns_ref, rows_ref, out_ref, back_ref
):
    kernel_count = kernels_ref.shape[1]
    band = kernels_ref.shape[3]

    def image(i):
        drive = (own_ref[i].astype(F32) + other_ref[i].astype(F32)).astype(BF)
        drive_twice = jnp.concatenate([drive, drive], axis=1)
        for k in range(kernel_count):
            push = drive_twice * fields_ref[i, k]
            back_ref[k] = dot(push, columns_ref[...]).astype(BF)
        total_real = total_imag = None
        for k in range(kernel_count):
            parts = dot(rows_ref[...], back_ref[k])
            spectral_real = parts[:band, :band] + parts[band:, band:]
            spectral_imag = parts[:band, band:] - parts[band:, :band]
            kernel_real = kernels_ref[0, k].astype(F32)
            kernel_imag = kernels_ref[1, k].astype(F32)
            term_real = kernel_real * spectral_real + kernel_imag * spectral_imag
            term_imag = kernel_real * spectral_imag - kernel_imag * spectral_real
            total_real = term_real if total_real is None else total_real + term_real
            total_imag = term_imag if total_imag is None else total_imag + term_imag
        scale = 0.25 * resist_gain
        out_ref[0, i] = (scale * total_real).astype(BF)
        out_ref[1, i] = (scale * total_imag).astype(BF)

    for_each(own_ref.shape[0], image)


def swap(value, axis, mask):
    count = lax.axis_size(axis)
    return lax.ppermute(value, axis, [(i, i ^ mask) for i in range(count)])


def add(first, *others):
    total = first.astype(F32)
    for other in others:
        total = total + other.astype(F32)
    return total.astype(BF)


def sum_axis(value, axis, unit, count):
    if count <= 4:
        return add(value, *[swap(value, axis, unit * m) for m in range(1, count)])
    bit = 1
    while bit < count:
        value = add(value, swap(value, axis, unit * bit))
        bit *= 2
    return value


def body(mask_theta, first_moment, second_moment, target_bits, kernels, kernel_weights):
    tile_count, row_count, column_count = mask_theta.shape
    word_count = target_bits.shape[2]
    band = kernels.shape[-1]
    coarse = 2 * band
    tiles = lax.axis_size("tile")
    chips = lax.axis_size("kern") // 2
    pixels = tiles * row_count
    strip = chips * column_count
    step = pixels // coarse
    tile_at = lax.axis_index("tile")
    kern_at = lax.axis_index("kern")
    core = kern_at % 2
    core_scalar = core.astype(jnp.int32).reshape(1)

    def after(values, anchor):
        return lax.optimization_barrier((values, anchor))[0]

    fine_table = jnp.asarray(cos_sin(band, pixels, np.arange(pixels)), BF)
    coarse_rows = cos_sin(band, pixels, np.arange(coarse) * step)
    cos_c, sin_c = coarse_rows[:, :band], coarse_rows[:, band:]
    field_rows = jnp.asarray(coarse_rows, BF)
    field_columns = jnp.asarray(
        np.block([[cos_c.T, sin_c.T], [-sin_c.T, cos_c.T]]) / band, BF
    )
    back_columns = jnp.asarray(np.block([[cos_c, -sin_c], [sin_c, cos_c]]) * (2.0 / band), BF)
    back_rows = jnp.asarray(coarse_rows.T, BF)
    up_table = jnp.asarray(interpolation(coarse, pixels), BF)
    place = np.arange(strip) % column_count
    padded = -(-word_count // 8) * 8
    word_of = (np.arange(strip) // column_count) * padded + place // 30
    bit_of = place % 30
    picks = jnp.asarray(
        (
            (np.arange(chips * padded)[None, :, None] == word_of)
            & (np.arange(4)[:, None, None] == bit_of // 8)
        ).reshape(4 * chips * padded, strip),
        BF,
    )
    shift = jnp.asarray((bit_of % 8)[None, :], jnp.int32)

    row_start = tile_at * row_count
    column_start = kern_at * column_count
    along_x = lax.dynamic_slice_in_dim(fine_table, row_start, row_count, 0)
    down_x = along_x.T
    across_y = lax.dynamic_slice_in_dim(fine_table, column_start, column_count, 0)
    onto_y = jnp.concatenate([across_y.T[:band], -across_y.T[band:]])

    def spread(shape, dtype=BF):
        return jax.ShapeDtypeStruct(shape, dtype)

    mine, theirs = call(
        functools.partial(mask_kernel, band, pixels),
        [spread((tile_count, band, band))] * 2,
        (mask_theta, across_y, down_x),
        scalars=(core_scalar,),
        flops=tile_count * 10**8,
    )
    mine = add(mine, swap(theirs, "kern", 1))

    scaled = (after(kernels, mine) * jnp.sqrt(kernel_weights)[None, :, None, None]).astype(BF)
    mine = sum_axis(mine, "kern", 2, chips)
    words = jnp.swapaxes(after(target_bits, mine), 1, 2)
    own_kernels = jnp.concatenate(
        [scaled] + [swap(scaled, "kern", 2 * m) for m in range(1, chips)], axis=1
    )
    kernel_count = own_kernels.shape[1]
    mine = sum_axis(mine, "tile", 1, tiles)
    trade = swap(mine, "kern", 1)
    pieces = jnp.stack([words] + [swap(words, "tile", m) for m in range(1, tiles)])
    pieces = jnp.stack([pieces] + [swap(pieces, "kern", 2 * m) for m in range(1, chips)])
    pieces = jnp.pad(pieces, [(0, 0)] * 3 + [(0, padded - word_count), (0, 0)])

    up_table_t = up_table.T
    starts = [(kern_at ^ (2 * m)) * column_count for m in range(chips)]
    up_y = jnp.concatenate(
        [lax.dynamic_slice_in_dim(up_table_t, at, column_count, 1) for at in starts], axis=1
    )
    down_y = jnp.concatenate(
        [lax.dynamic_slice_in_dim(up_table, at, column_count, 0) for at in starts], axis=0
    )

    groups = []
    for size in GROUPS:
        start = groups[-1].stop if groups else 0
        groups.append(slice(start, min(start + size, tile_count)))

    def unpack(anchor):
        everything = call(
            unpack_kernel,
            [spread((group.stop - group.start, pixels, strip)) for group in groups],
            (after(pieces, anchor), picks, shift),
            scalars=(tile_at.astype(jnp.int32).reshape(1),),
            flops=6 * 10**8,
        )
        return everything

    signs = []

    steps = range(first_step, first_step + ITERS)
    fixes = jnp.asarray([[1.0 - beta_one**s, 1.0 - beta_two**s] for s in steps], F32)

    def traded(values):
        return [(value, after(swap(value, "kern", 1), values[-1])) for value in values]

    def adjoints(mine, trade):
        counts = [group.stop - group.start for group in groups]
        fields, values = [], []
        for group, count in zip(groups, counts):
            field, intensity = call(
                field_kernel,
                [
                    spread((count, kernel_count, coarse, 2 * coarse)),
                    spread((count, coarse, coarse)),
                ],
                (mine[group], trade[group], own_kernels, field_rows, field_columns),
                scalars=(core_scalar,),
                scratch=[pltpu.VMEM((kernel_count, coarse, coarse), BF)],
                flops=count * 10**9,
            )
            fields.append(field)
            values.append(intensity)
        if not signs:
            signs.extend(unpack(values[-1]))
        values = [
            call(
                resist_kernel,
                spread((count, coarse, coarse)),
                (*pair, sign, up_table, up_table_t, up_y, down_y),
                scratch=[pltpu.VMEM((pixels, strip), BF)],
                flops=count * 7 * 10**8,
            )
            for count, pair, sign in zip(counts, traded(values), signs)
        ]
        values = [
            call(
                adjoint_kernel,
                spread((2, count, band, band)),
                (*pair, field, own_kernels, back_columns, back_rows),
                scratch=[pltpu.VMEM((kernel_count, coarse, coarse), BF)],
                flops=count * 10**9,
            )
            for count, pair, field in zip(counts, traded(values), fields)
        ]
        return sum([[value, swap(value, "kern", 1)] for value in values], [])

    block = spread(mask_theta.shape, F32)
    half = spread((tile_count, band, band))
    state = [mask_theta, first_moment, second_moment]
    for iteration in range(ITERS):
        last = iteration == ITERS - 1
        pairs = adjoints(mine, trade)
        outs = call(
            functools.partial(update_kernel, band, pixels, last),
            [block] * 3 + ([block] if last else [half] * 2),
            (*pairs, *state, along_x, onto_y, across_y, down_x),
            scalars=(core_scalar, fixes[iteration]),
            scratch=[pltpu.VMEM((2, tile_count, band, band), BF)],
            flops=6 * 10**8,
        )
        if last:
            return tuple(outs)
        state, (mine, theirs) = outs[:3], outs[3:]
        mine = add(mine, swap(theirs, "kern", 1))
        mine = sum_axis(mine, "kern", 2, chips)
        mine = sum_axis(mine, "tile", 1, tiles)
        trade = swap(mine, "kern", 1)


def solution(mesh):
    block = P("grp", "tile", "kern")
    return jax.shard_map(
        body,
        mesh=mesh,
        in_specs=(block, block, block, block, P(None, "kern", None, None), P("kern")),
        out_specs=(block, block, block, block),
        check_vma=False,
    )
```
